128 devices in a mesh: patch: 16 (over z, y), body: 8 (over x, core).
Axes of the slice: x: 4, y: 4, z: 4, core: 2. Of those that a mesh axis runs over, the one named last changes fastest.
Arguments:
- donors: bfloat16 [120, 262144], P(None, ('patch', 'body')), may hold values from -3 to 3
- owner: int32 [262144, 1], P(('patch', 'body')), may hold values from 0 to 127; in each aligned block of 2048 rows (0 to 2047, 2048 to 4095, ...) at most 32 rows name the same one
- slot: int32 [262144], P(('patch', 'body')), may hold values from 0 to 255
- target: float32 [32, 1024, 3], P('patch', 'body'), may hold values from -6 to 6
- weight_a: bfloat16 [3, 5, 96], replicated, may hold values from -1.5 to 1.5
- weight_b: bfloat16 [9, 96, 96], replicated, may hold values from -0.21875 to 0.21875
- weight_h: bfloat16 [2304, 3], replicated, may hold values from -0.125 to 0.125
Outputs:
- stress: float32 [32, 1024, 3], P('patch', 'body')
- profile_grad: float32 [120, 32, 1024], P(None, 'patch', 'body')
- grad_a: float32 [3, 5, 96], replicated
- grad_b: float32 [9, 96, 96], replicated
- grad_h: float32 [2304, 3], replicated
The draws below stay inside these ranges and needn't reach their ends.
Inputs may be any that keep to these rules, and one draw needn't show every extreme that they name: Of the donor rows of one device, at most 32 name the same owner; some owner gets exactly 32 from some device.
All inputs are finite; a program needn't handle non-finite values.
Results may differ from the reference program's by a relative error of at most 0.006.
Values may be sent and summed in bfloat16 or wider, within the bound.
No kernel may reach another device: no remote copies, remote signals or barrier semaphores. Data moves between devices by JAX's collectives and lax.ppermute only.
A program may use at most 128 MiB of HBM per device.

```python
import math
import jax
import jax.numpy as jnp
import numpy as np
from jax import lax

C = 96
H = 24
F = 5
TX = 2
TY = 128
HF = 120
DON_DEV = 2048
NDON = 262144
CAP = 32
WX = 32
WY = 1024
N_PATCH = 16
N_BODY = 8
DEVICES = 128


def set_ends(drawn, key, least, largest):
    longest = drawn.shape.index(max(drawn.shape))
    spots = []
    for shift in (0, 1):
        where = [jax.random.randint(jax.random.fold_in(key, axis), (), 0, length) for axis, length in enumerate(drawn.shape)]
        where[longest] = (where[longest] + shift) % drawn.shape[longest]
        spots.append(tuple(where))
    return drawn.at[spots[0]].set(least).at[spots[1]].set(largest)


def shard_levels(own_key, extent, split, low, high):
    gain = 1.0
    for axis_at, parts in split:
        steps = jax.random.uniform(jax.random.fold_in(jax.random.fold_in(own_key, 6), axis_at), (parts,), jnp.float32, low / len(split), high / len(split))
        gain = gain * jnp.repeat(jnp.exp(steps), extent[axis_at] // parts).reshape((-1,) + (1,) * (len(extent) - 1 - axis_at))
    return gain


def deal_out(rng, own, number, rows, amount, top, limit, lean):
    sequence = jax.random.permutation(rng, amount)
    packed, common = shares(amount, rows * top, limit, lean, True), shares(amount, rows * top, limit, lean, False)
    places = jnp.arange(amount)

    def named(sizes, turn):
        used = int((sizes > 0).sum())
        fixed = max(1, used // 4)
        passed = fixed + (places - fixed + turn * (used - fixed)) % max(1, amount - fixed)
        return jnp.zeros((amount,), jnp.int32).at[sequence[jnp.where(places < fixed, places, passed)]].set(jnp.asarray(sizes, jnp.int32))

    sizes = jnp.where(number % 4 == 0, named(packed, number // 4), named(common, number - number // 4 - 1))
    mixed = jax.random.permutation(jax.random.fold_in(own, 3), amount)
    donor, receiver = mixed[0:amount // 2 * 2:2], mixed[1:amount // 2 * 2:2]
    room = jnp.minimum(sizes[donor] - 1, limit - sizes[receiver]) // 2
    room = jnp.where((donor == sequence[0]) | (receiver == sequence[0]) | (sizes[receiver] == 0), 0, jnp.maximum(room, 0))
    passed = jax.random.randint(jax.random.fold_in(own, 4), (amount // 2,), 0, 1 << 20) % (room + 1)
    sizes = sizes.at[donor].add(-passed).at[receiver].add(passed)
    members = jnp.searchsorted(jnp.cumsum(sizes), jnp.arange(rows * top), side="right").astype(jnp.int32)
    listing = members.reshape(top, rows).T
    listing = listing[jax.random.permutation(jax.random.fold_in(own, 1), rows)]
    turn = jax.random.randint(jax.random.fold_in(own, 2), (rows, 1), 0, top)
    return jnp.take_along_axis(listing, (jnp.arange(top)[None, :] + turn) % top, axis=1)


def shares(amount, total, reach, skew, full):
    portions = [(1 << 20) // math.isqrt(grade ** skew) + 1 for grade in range(1, amount + 1)]
    largest = reach if full else min(reach, max(-(-total // amount), total * portions[0] // sum(portions)))
    least = 1 if total - largest >= amount - 1 else 0
    given, spare = [largest] + [least] * (amount - 1), total - largest - least * (amount - 1)
    while spare > 0:
        candidates = [i for i in range(1, amount) if given[i] < largest] or [i for i in range(1, amount) if given[i] < reach]
        pool, remaining = sum([portions[i] for i in candidates]), spare
        for i in candidates:
            extra = min(reach - given[i], max(1, remaining * portions[i] // pool), spare)
            given[i] = given[i] + extra
            spare = spare - extra
    return np.array(given)


def bell_draw(rng, dims, width, reach, shards=(), kind=jnp.bfloat16):
    array = width * jax.random.normal(rng, dims, jnp.float32)
    if shards:
        array = array * shard_levels(rng, dims, shards, -0.22, 0.18)
    return jnp.clip(array, -reach, reach).astype(kind)


def setup_inputs(seed: int = 0) -> dict:
    streams_of = jax.random.split(jax.random.key(seed), 8)
    donors = bell_draw(streams_of[0], (HF, NDON), 0.35, 3.0, ((1, 128),))
    owner_keys = jax.random.split(jax.random.fold_in(streams_of[1], 1), NDON // DON_DEV)
    owner_turns = jax.random.permutation(jax.random.fold_in(streams_of[1], 3), NDON // DON_DEV)
    owner = jax.vmap(lambda own, number: deal_out(jax.random.fold_in(streams_of[1], 2), own, number, DON_DEV, DEVICES, 1, CAP, 2))(owner_keys, owner_turns).reshape((NDON, 1))
    slot = set_ends(jax.random.randint(streams_of[2], (NDON,), 0, TX * TY), jax.random.fold_in(streams_of[2], 1), 0, (TX * TY) - 1).astype(jnp.int32)
    target = bell_draw(streams_of[3], (WX, WY, 3), 1.0, 6.0, ((0, 16), (1, 8)), jnp.float32)
    weight_a = bell_draw(streams_of[4], (3, F, C), (3 * F) ** -0.5, 1.5)
    weight_b = bell_draw(streams_of[5], (9, C, C), (9 * C) ** -0.5, 0.21875)
    weight_h = bell_draw(streams_of[6], (H * C, 3), (H * C) ** -0.5, 0.125)
    return dict(donors=donors, owner=owner, slot=slot, target=target, weight_a=weight_a, weight_b=weight_b, weight_h=weight_h)


def silu_slope(value):
    sig = jax.nn.sigmoid(value)
    return sig * (1.0 + value * (1.0 - sig))

def reference(donors, owner, slot, target, weight_a, weight_b, weight_h):
    wide_x = TX * N_PATCH
    wide_y = TY * N_BODY
    points = wide_x * wide_y
    dest = owner[:, 0]
    grid_x = (dest // N_BODY * TX + slot // TY).astype(jnp.int32)
    grid_y = (dest % N_BODY * TY + slot % TY).astype(jnp.int32)
    summed = jnp.zeros((wide_x, wide_y, H * F), jnp.float32).at[grid_x, grid_y].add(jnp.transpose(donors).astype(jnp.float32))
    profile = summed.astype(jnp.bfloat16).reshape(wide_x, wide_y, H, F)
    profile_pad = jnp.pad(profile, ((0, 0), (0, 0), (2, 2), (0, 0)))
    kernel_a = weight_a.reshape(3 * F, C)
    head = weight_h.reshape(H, C, 3)

    def unfold_at(height):
        rows = lax.dynamic_slice_in_dim(profile_pad, height, 5, axis=2)
        return jnp.concatenate([rows[:, :, 0], rows[:, :, 2], rows[:, :, 4]], axis=2).reshape(points, 3 * F)

    def forward_at(height):
        unfold = unfold_at(height)
        pre_a = jnp.dot(unfold, kernel_a, preferred_element_type=jnp.float32)
        act_one = jax.nn.silu(pre_a).astype(jnp.bfloat16)
        padded = jnp.pad(act_one.reshape(wide_x, wide_y, C), ((1, 1), (1, 1), (0, 0)))
        pre_b = jnp.zeros((points, C), jnp.float32)
        for tap in range(9):
            shift_x, shift_y = (tap // 3, tap % 3)
            piece = padded[shift_x:shift_x + wide_x, shift_y:shift_y + wide_y].reshape(points, C)
            pre_b = pre_b + jnp.dot(piece, weight_b[tap], preferred_element_type=jnp.float32)
        act_two = (act_one.astype(jnp.float32) + jax.nn.silu(pre_b)).astype(jnp.bfloat16)
        return (unfold, pre_a, act_one, padded, pre_b, act_two)

    def stress_at(height):
        act_two = forward_at(height)[5]
        return jnp.dot(act_two, head[height], preferred_element_type=jnp.float32)
    heights = jnp.arange(H, dtype=jnp.int32)
    stress = lax.optimization_barrier(jnp.sum(lax.map(stress_at, heights), axis=0))
    err = (stress - target.reshape(points, 3)).astype(jnp.bfloat16)
    contract_rows = (((0,), (0,)), ((), ()))
    contract_cols = (((1,), (1,)), ((), ()))

    def backward_at(height):
        unfold, pre_a, act_one, padded, pre_b, act_two = forward_at(height)
        part_h = lax.dot_general(act_two, err, contract_rows, preferred_element_type=jnp.float32)
        dz_two = lax.dot_general(err, head[height], contract_cols, preferred_element_type=jnp.float32)
        da_two = (dz_two * silu_slope(pre_b)).astype(jnp.bfloat16)
        da_pad = jnp.pad(da_two.reshape(wide_x, wide_y, C), ((1, 1), (1, 1), (0, 0)))
        parts_b = []
        dz_one = dz_two
        for tap in range(9):
            shift_x, shift_y = (tap // 3, tap % 3)
            piece = padded[shift_x:shift_x + wide_x, shift_y:shift_y + wide_y].reshape(points, C)
            parts_b.append(lax.dot_general(piece, da_two, contract_rows, preferred_element_type=jnp.float32))
            back = da_pad[2 - shift_x:2 - shift_x + wide_x, 2 - shift_y:2 - shift_y + wide_y].reshape(points, C)
            dz_one = dz_one + lax.dot_general(back, weight_b[tap], contract_cols, preferred_element_type=jnp.float32)
        da_one = (dz_one * silu_slope(pre_a)).astype(jnp.bfloat16)
        part_a = lax.dot_general(unfold, da_one, contract_rows, preferred_element_type=jnp.float32)
        spread = jnp.stack([lax.dot_general(da_one, weight_a[tap], contract_cols, preferred_element_type=jnp.float32) for tap in range(3)])
        return (part_h, jnp.stack(parts_b), part_a, spread)
    parts_h, parts_b, parts_a, spreads = lax.map(backward_at, heights)
    collect = jnp.zeros((H + 4, points, F), jnp.float32)
    for tap in range(3):
        collect = collect.at[2 * tap:2 * tap + H].add(spreads[:, tap])
    profile_grad = jnp.transpose(collect[2:2 + H], (1, 0, 2)).reshape(wide_x, wide_y, H * F)
    profile_grad = jnp.transpose(profile_grad, (2, 0, 1))
    scale = 1.0 / jnp.sqrt(jnp.float32(points))
    grad_a = (lax.optimization_barrier(jnp.sum(parts_a, axis=0)) * scale).reshape(3, F, C)
    grad_b = lax.optimization_barrier(jnp.sum(parts_b, axis=0)) * scale
    grad_h = parts_h.reshape(H * C, 3) * scale
    return (stress.reshape(wide_x, wide_y, 3), profile_grad, grad_a, grad_b, grad_h)
```

```python
import functools

import jax
import jax.numpy as jnp
from jax import lax
from jax.experimental import pallas as pl
from jax.experimental.pallas import tpu as pltpu
from jax.sharding import PartitionSpec as P

F32 = jnp.float32
BF16 = jnp.bfloat16
AXES = ("patch", "body")
C = 96
H = 24
F = 5
V = H * F
TX = 2
TY = 128
S = TY + 4
Q = 896
LO, HI = 128, 768
OLO, OHI = 256, 640
NA = HI - LO
NO = OHI - OLO
OWN = (2 * S + 2, 3 * S + 2)
TAPS = tuple((di - 1) * S + (dj - 1) for di in range(3) for dj in range(3))
KB = 9 * C
COLS = (((1,), (1,)), ((), ()))
LIMIT = 60 * 1024 * 1024


def dot(a, b):
    return jnp.dot(a, b, preferred_element_type=F32)


def dot_t(a, b):
    return lax.dot_general(a, b, COLS, preferred_element_type=F32)


def iota(shape, dim):
    return lax.broadcasted_iota(jnp.int32, shape, dim)


def pack_kernel(cap, donors, owner, slot, out, dext, place):
    rows = donors.shape[1]
    n_dev = 128
    dext[0:V, :] = donors[...]
    pad = iota((8, rows), 0)
    dext[V : V + 8, :] = jnp.where(pad == 0, slot[...], 0).astype(F32).astype(BF16)
    wide = 256
    upper = (iota((wide, wide), 0) < iota((wide, wide), 1)).astype(F32).astype(BF16)
    carry = jnp.zeros((n_dev, 1), F32)
    for at in range(0, rows, wide):
        dest = owner[:, at : at + wide]
        hit = (iota((n_dev, wide), 0) == dest).astype(F32)
        before = dot(hit.astype(BF16), upper) + carry
        rank = jnp.sum(before * hit, axis=0, keepdims=True)
        carry = carry + jnp.sum(hit, axis=1, keepdims=True)
        place[:, at : at + wide] = dest * cap + rank.astype(jnp.int32)
    block = 256

    def step(n, _):
        base = n * block
        pick = (iota((block, rows), 0) == place[...] - base).astype(F32).astype(BF16)
        out[pl.ds(pl.multiple_of(base, block), block), :] = dot_t(pick, dext[...]).astype(BF16)
        return 0

    lax.fori_loop(0, n_dev * cap // block, step, 0)


def unpack_kernel(inbox, target, prof, left, right, side):
    total = inbox.shape[0]
    points = TX * TY
    lane = iota((8, 128), 1)
    mark = (lane == V).astype(F32).astype(BF16)
    acc = jnp.zeros((points, 128), F32)
    chunk = 1024
    for at in range(0, total, chunk):
        rows = inbox[at : at + chunk, :]
        slots = dot_t(mark, rows)[0:1, :].astype(jnp.int32)
        pick = (iota((points, chunk), 0) == slots).astype(F32).astype(BF16)
        acc = acc + dot(pick, rows)
    acc = jnp.where(iota((points, 128), 1) < V, acc, 0.0)
    for r in range(TX):
        goal = target[:, r, :]
        high = goal.astype(BF16).astype(F32)
        rest = goal - high
        side[...] = jnp.zeros((128, 128), F32)
        side[V : V + 3, :] = high
        side[V + 3 : V + 6, :] = rest
        part = acc[r * TY : (r + 1) * TY, :] + jnp.transpose(side[...])
        prof[r * TY : (r + 1) * TY, :] = part.astype(BF16)
        if r == 0:
            keep = part
    side[0:2, :] = keep[0:2, :]
    side[2:4, :] = part[0:2, :]
    side[4:16, :] = jnp.zeros((12, 128), F32)
    left[...] = side[0:16, :].astype(BF16)
    side[0:2, :] = keep[TY - 2 : TY, :]
    side[2:4, :] = part[TY - 2 : TY, :]
    right[...] = side[0:16, :].astype(BF16)


def step_kernel(own, upper, lower, wa, wat, wf, wb, wh, wht, sel, stress_out, pgrad, grads,
                ext, prof, unf, zc, u1s, u2s, z2s, dac, da1s, err_s, gb):
    ext[S * 6 : Q, :] = jnp.zeros((Q - S * 6, 128), F32)
    for row, src in ((0, upper), (2, own), (4, lower)):
        block = src[...].astype(F32)
        for r in range(TX):
            at = (row + r) * S
            ext[at : at + 2, :] = block[256 + 2 * r : 258 + 2 * r, :]
            ext[at + 2 : at + 2 + TY, :] = block[r * TY : (r + 1) * TY, :]
            ext[at + 2 + TY : at + S, :] = block[272 + 2 * r : 274 + 2 * r, :]
    wide = jnp.transpose(ext[...])
    prof[...] = wide.astype(BF16)
    goal = wide[V : V + 8, LO:HI]
    goal = goal + jnp.concatenate([goal[3:8], goal[0:3]], axis=0)

    lane = iota((8, NA), 1) + LO
    row_at = lane // S
    col_at = lane - row_at * S
    grid_x = lax.axis_index("patch") * TX + row_at - 2
    grid_y = lax.axis_index("body") * TY + col_at - 2
    width_x = lax.axis_size("patch") * TX
    width_y = lax.axis_size("body") * TY
    ring = (row_at >= 1) & (row_at <= 4) & (col_at >= 1) & (col_at <= S - 2)
    inside = (grid_x >= 0) & (grid_x < width_x) & (grid_y >= 0) & (grid_y < width_y)
    mine = (row_at >= 2) & (row_at <= 3) & (col_at >= 2) & (col_at <= S - 3)
    ring_mask = (ring & inside & (iota((8, NA), 0) < 3)).astype(F32)
    own_mask = mine.astype(F32)

    def forward(h, _):
        u1 = dot(wa[h], prof[...])
        z1f = u1 + u1 * jnp.tanh(u1)
        z1 = z1f.astype(BF16)
        u1s[h] = u1[:, OLO:OHI]
        z1c = z1f.astype(BF16).astype(F32)
        for tap, shift in enumerate(TAPS):
            moved = z1c if shift == 0 else pltpu.roll(z1c, (-shift) % Q, 1)
            zc[h, tap * C : (tap + 1) * C, :] = moved[:, LO:HI].astype(BF16)
        u2 = dot(wf[...], zc[h])
        u2s[h] = u2
        act = z1c[:, LO:HI] + (u2 + u2 * jnp.tanh(u2))
        z2s[h] = act.astype(BF16)
        return 0

    lax.fori_loop(0, H, forward, 0)
    z2 = z2s[...].reshape(H * C, NA)
    stress = dot(wh[...], z2)
    for r in range(TX):
        at = OWN[r] - LO
        stress_out[:, r, :] = stress[0:3, at : at + TY]
    err = ((stress - goal) * ring_mask).astype(BF16)
    err_s[...] = err
    err_own = (err[:, OLO - LO : OHI - LO].astype(F32) * own_mask[:, OLO - LO : OHI - LO]).astype(BF16)
    grad_h = dot_t(err_own, z2s[:, :, OLO - LO : OHI - LO].reshape(H * C, NO))
    for t in range(H * C // 128):
        grads[108 + t] = grad_h[:, t * 128 : (t + 1) * 128]
    own_wide = jnp.broadcast_to(own_mask[0:1, OLO - LO : OHI - LO], (C, NO))
    own_prof = (prof[:, OLO:OHI].astype(F32) * own_mask[0:1, OLO - LO : OHI - LO]).astype(BF16)
    unf[...] = dot(sel[...], own_prof).astype(BF16).reshape(H, 16, NO)
    gb[...] = jnp.zeros_like(gb)

    def backward(h, grad_a):
        u2 = u2s[h]
        t2 = jnp.tanh(u2)
        dz2 = dot(wht[h], err_s[...])
        da2 = (dz2 * ((1.0 + t2) * (1.0 + u2 * (1.0 - t2)))).astype(BF16)
        da2f = da2.astype(F32)
        mid = (da2f[:, OLO - LO : OHI - LO] * own_wide).astype(BF16)
        gb[...] += dot_t(mid, zc[h, :, OLO - LO : OHI - LO])
        for tap, shift in enumerate(TAPS):
            moved = da2f if shift == 0 else pltpu.roll(da2f, shift % NA, 1)
            dac[tap * C : (tap + 1) * C, :] = moved[:, OLO - LO : OHI - LO].astype(BF16)
        dz1 = dz2[:, OLO - LO : OHI - LO] + dot(wb[...], dac[...])
        u1 = u1s[h]
        t1 = jnp.tanh(u1)
        da1 = (dz1 * ((1.0 + t1) * (1.0 + u1 * (1.0 - t1)))).astype(BF16)
        da1s[h] = da1
        return grad_a + dot_t(unf[h], da1)

    grad_a = lax.fori_loop(0, H, backward, jnp.zeros((16, C), F32))
    blank = jnp.zeros((16, 128 - C), F32)
    grad_a = jnp.concatenate([grad_a, blank], axis=1)
    grads[126] = grad_a[0:8]
    grads[127] = grad_a[8:16]
    grad_b = jnp.transpose(gb[...])
    blank = jnp.zeros((KB, 128 - C), F32)
    grads[0:108] = jnp.concatenate([grad_b, blank], axis=1).reshape(108, 8, 128)
    back = dot(wat[...], da1s[...].reshape(H * C, NO))
    for r in range(TX):
        at = OWN[r] - OLO
        pgrad[:, r, :] = back[0:V, at : at + TY]


def spread_kernel(sums, grad_a, grad_b, grad_h):
    for tap in range(9):
        rows = sums[12 * tap : 12 * (tap + 1)].astype(F32).reshape(C, 128)
        grad_b[tap] = rows[:, 0:C]
    for t in range(H * C // 128):
        grad_h[:, t * 128 : (t + 1) * 128] = sums[108 + t].astype(F32)[0:3]
    low = sums[126].astype(F32)[:, 0:C]
    high = sums[127].astype(F32)[:, 0:C]
    for k in range(3):
        for f in range(F):
            n = k * F + f
            grad_a[f, k : k + 1, :] = low[n : n + 1] if n < 8 else high[n - 8 : n - 7]


def call(kernel, out_shape, scratch=()):
    return pl.pallas_call(
        kernel,
        out_shape=out_shape,
        scratch_shapes=list(scratch),
        compiler_params=pltpu.CompilerParams(vmem_limit_bytes=LIMIT),
    )


def shape(dims, kind):
    return jax.ShapeDtypeStruct(dims, kind)


def exchange(blocks):
    return lax.all_to_all(blocks, AXES, split_axis=0, concat_axis=0, tiled=True)


def shards(donors, owner, slot, target, weight_a, weight_b, weight_h):
    n_patch = lax.axis_size("patch")
    n_body = lax.axis_size("body")
    n_dev = n_patch * n_body
    rows = donors.shape[1]
    cap = 2 * rows // n_dev
    outbox = call(
        functools.partial(pack_kernel, cap),
        shape((n_dev * cap, 128), BF16),
        [pltpu.VMEM((128, rows), BF16), pltpu.VMEM((1, rows), jnp.int32)],
    )(donors, owner.reshape(1, rows), slot.reshape(1, rows))
    inbox = exchange(outbox.reshape(n_dev, cap, 128)).reshape(n_dev * cap, 128)

    half = jnp.asarray(0.5, BF16)
    heights = jnp.arange(H)
    reach = heights[None, :, None] + 2 * (jnp.arange(3)[:, None, None] - 1) == heights[None, None, :]
    band = jnp.einsum("khg,kfc->hcgf", reach.astype(BF16), weight_a).reshape(H * C, V)
    band = jnp.pad(band, ((0, 0), (0, 128 - V)))
    wa = (band * half).reshape(H, C, 128)
    wat = jnp.transpose(band)
    wf = jnp.transpose(weight_b, (2, 0, 1)).reshape(C, KB) * half
    wb = jnp.transpose(weight_b, (1, 0, 2)).reshape(C, KB) * half
    wh = jnp.pad(jnp.transpose(weight_h), ((0, 5), (0, 0)))
    wht = (jnp.pad(weight_h, ((0, 0), (0, 5))) * half).reshape(H, C, 8)
    line = jnp.arange(16)
    want = (heights[:, None] + 2 * (line[None, :] // F - 1)) * F + line[None, :] % F
    sel = (want[:, :, None] == jnp.arange(128)[None, None, :]) & (want >= 0)[:, :, None]
    sel = sel & (want < V)[:, :, None] & (line < 15)[None, :, None]
    sel = sel.astype(BF16).reshape(H * 16, 128)

    prof, left, right = call(
        unpack_kernel,
        (shape((TX * TY, 128), BF16), shape((16, 128), BF16), shape((16, 128), BF16)),
        [pltpu.VMEM((128, 128), F32)],
    )(inbox, jnp.transpose(target, (2, 0, 1)))
    fore = [(i, i + 1) for i in range(n_body - 1)]
    back = [(i + 1, i) for i in range(n_body - 1)]
    from_left = lax.ppermute(right, "body", fore)
    from_right = lax.ppermute(left, "body", back)
    tile = jnp.concatenate([prof, from_left, from_right], axis=0)
    fore = [(i, i + 1) for i in range(n_patch - 1)]
    back = [(i + 1, i) for i in range(n_patch - 1)]
    above = lax.ppermute(tile, "patch", fore)
    below = lax.ppermute(tile, "patch", back)

    stress, pgrad, grads = call(
        step_kernel,
        (shape((3, TX, TY), F32), shape((V, TX, TY), F32), shape((128, 8, 128), F32)),
        [
            pltpu.VMEM((Q, 128), F32),
            pltpu.VMEM((128, Q), BF16),
            pltpu.VMEM((H, 16, NO), BF16),
            pltpu.VMEM((H, KB, NA), BF16),
            pltpu.VMEM((H, C, NO), F32),
            pltpu.VMEM((H, C, NA), F32),
            pltpu.VMEM((H, C, NA), BF16),
            pltpu.VMEM((KB, NO), BF16),
            pltpu.VMEM((H, C, NO), BF16),
            pltpu.VMEM((8, NA), BF16),
            pltpu.VMEM((C, KB), F32),
        ],
    )(tile, above, below, wa, wat, wf, wb, wh, wht, sel)
    scale = 1.0 / jnp.sqrt(jnp.float32(TX * TY * n_dev))
    total = (jnp.sum(exchange(grads), axis=0) * scale).astype(BF16)
    sums = exchange(jnp.broadcast_to(total[None], (n_dev, 8, 128)))
    grad_a, grad_b, grad_h = call(
        spread_kernel,
        (shape((F, 3, C), F32), shape((9, C, C), F32), shape((3, H * C), F32)),
    )(sums)
    return (
        jnp.transpose(stress, (1, 2, 0)),
        pgrad,
        jnp.transpose(grad_a, (1, 0, 2)),
        grad_b,
        jnp.transpose(grad_h),
    )


def solution(mesh):
    placed = (
        P(None, ("patch", "body")),
        P(("patch", "body"), None),
        P(("patch", "body")),
        P("patch", "body", None),
        P(),
        P(),
        P(),
    )
    return jax.shard_map(
        shards,
        mesh=mesh,
        in_specs=placed,
        out_specs=(P("patch", "body", None), P(None, "patch", "body"), P(), P(), P()),
        check_vma=False,
    )
```

```python
import functools

import jax
import jax.numpy as jnp
from jax import lax
from jax.experimental import pallas as pl
from jax.experimental.pallas import tpu as pltpu
from jax.sharding import PartitionSpec as P

F32 = jnp.float32
BF16 = jnp.bfloat16
AXES = ("patch", "body")
C = 96
H = 24
F = 5
V = H * F
TX = 2
TY = 128
ROWS = TX + 4
NZ = ROWS + 1
NA = ROWS - 1
Q = NZ * TY
KB = 9 * C
BESIDE = tuple((di - 1) * 8 + (dj - 1) * 2 for di in range(3) for dj in range(3))
COLS = (((1,), (1,)), ((), ()))
MIB = 1024 * 1024


def dot(a, b):
    return jnp.dot(a, b, preferred_element_type=F32)


def dot_t(a, b):
    return lax.dot_general(a, b, COLS, preferred_element_type=F32)


def iota(shape, dim):
    return lax.broadcasted_iota(jnp.int32, shape, dim)


def pack_kernel(cap, donors_far, owner_far, slot_far, out, dext, owner, slot, place, sems):
    rows = donors_far.shape[1]
    n_dev = 128
    own_copy = pltpu.make_async_copy(owner_far, owner, sems.at[0])
    slot_copy = pltpu.make_async_copy(slot_far, slot, sems.at[1])
    donor_copy = pltpu.make_async_copy(donors_far, dext.at[0:V], sems.at[2])
    own_copy.start()
    slot_copy.start()
    donor_copy.start()
    own_copy.wait()
    part = 256
    upper = (iota((part, part), 0) < iota((part, part), 1)).astype(F32).astype(BF16)
    carry = jnp.zeros((n_dev, 1), F32)
    spots = []
    for at in range(0, rows, part):
        dest = owner[:, at : at + part]
        hit = (iota((n_dev, part), 0) == dest).astype(F32)
        before = dot(hit.astype(BF16), upper) + carry
        rank = jnp.sum(before * hit, axis=0, keepdims=True)
        carry = carry + jnp.sum(hit, axis=1, keepdims=True)
        spot = (dest * cap).astype(F32) + rank
        spots += [spot[:, 0:128], spot[:, 128:256]]
    tall = jnp.transpose(jnp.concatenate(spots, axis=0))
    for n in range(rows // 128):
        place[n * 128 : (n + 1) * 128, :] = jnp.broadcast_to(tall[:, n : n + 1], (128, 128))
    slot_copy.wait()
    pad = iota((8, rows), 0)
    dext[V : V + 8, :] = jnp.where(pad == 0, slot[...], 0).astype(F32).astype(BF16)
    donor_copy.wait()
    block = 256
    marks = [(iota((1, 128), 1) + 128 * t).astype(F32).astype(BF16) for t in range(2)]

    one, none = jnp.asarray(1.0, BF16), jnp.asarray(0.0, BF16)

    def step(n, _):
        for m in range(2):
            base = (2 * n + m) * block
            spot = (place[...] - base.astype(F32)).astype(BF16)
            pick = jnp.concatenate([jnp.where(spot == mark, one, none) for mark in marks], axis=1)
            picked = dot(dext[...], pick)
            out[pl.ds(pl.multiple_of(base, block), block), :] = jnp.transpose(picked).astype(BF16)
        return 0

    lax.fori_loop(0, n_dev * cap // block // 2, step, 0)


def unpack_kernel(inbox, target, prof, left, right, side):
    total = inbox.shape[0]
    points = TX * TY
    lane = iota((8, 128), 1)
    mark = (lane == V).astype(F32).astype(BF16)
    acc = jnp.zeros((points, 128), F32)
    chunk = 1024
    for at in range(0, total, chunk):
        rows = inbox[at : at + chunk, :]
        slots = dot_t(mark, rows)[0:1, :].astype(jnp.int32)
        pick = (iota((points, chunk), 0) == slots).astype(F32).astype(BF16)
        acc = acc + dot(pick, rows)
    acc = jnp.where(iota((points, 128), 1) < V, acc, 0.0)
    for r in range(TX):
        goal = target[:, r, :]
        high = goal.astype(BF16).astype(F32)
        rest = goal - high
        side[...] = jnp.zeros((128, 128), F32)
        side[V : V + 3, :] = high
        side[V + 3 : V + 6, :] = rest
        part = acc[r * TY : (r + 1) * TY, :] + jnp.transpose(side[...])
        prof[r * TY : (r + 1) * TY, :] = part.astype(BF16)
        if r == 0:
            keep = part
    side[0:2, :] = keep[0:2, :]
    side[2:4, :] = part[0:2, :]
    side[4:16, :] = jnp.zeros((12, 128), F32)
    left[...] = side[0:16, :].astype(BF16)
    side[0:2, :] = keep[TY - 2 : TY, :]
    side[2:4, :] = part[TY - 2 : TY, :]
    right[...] = side[0:16, :].astype(BF16)


def turned(tile, shift):
    return tile if shift == 0 else pltpu.roll(tile, (-shift) % TY, 1)


def three(tile, beside, row):
    ends = turned(beside, 8 * row + 3)
    lane = iota((C, TY), 1)
    return (
        jnp.where(lane == 0, ends, turned(tile, -1)),
        tile,
        jnp.where(lane == TY - 1, ends, turned(tile, 1)),
    )


def wide_of(tiles):
    return jnp.concatenate(list(tiles), axis=1)


def step_kernel(own, first, second, wa, wat, wf, wb, wh, wht, sel, stress_out, pgrad, grads,
                ext, prof, unf, zs, zb, u1s, u2s, z2s, das, dzs, da1s, err_s, gb):
    patch = lax.axis_index("patch")
    body = lax.axis_index("body")
    odd_x = patch % 2 == 1
    odd_y = body % 2 == 1
    has_left = jnp.where(body > 0, 1.0, 0.0)
    has_right = jnp.where(body < lax.axis_size("body") - 1, 1.0, 0.0)
    has_up = jnp.where(patch > 0, 1.0, 0.0)
    has_down = jnp.where(patch < lax.axis_size("patch") - 1, 1.0, 0.0)
    ext[...] = jnp.zeros((128, 128), F32)
    goals = []
    one, two = first[...].astype(F32), second[...].astype(F32)
    sources = (
        jnp.where(odd_x, one, two) * has_up,
        own[...].astype(F32),
        jnp.where(odd_x, two, one) * has_down,
    )
    for row in range(ROWS):
        src, r = sources[row // TX], row % TX
        block = src[r * TY : (r + 1) * TY, :]
        one, two = src[256:288], src[288:320]
        left = jnp.where(odd_y, one, two)[16 + 2 * r : 18 + 2 * r] * has_left
        right = jnp.where(odd_y, two, one)[2 * r : 2 * r + 2] * has_right
        parts = (block[TY - 1 : TY], left[0:1], right[0:1], left[1:2], right[1:2], block[0:1])
        for n, part in enumerate(parts):
            ext[8 * row + n : 8 * row + n + 1, :] = part
        wide = jnp.transpose(block)
        prof[:, row * TY : (row + 1) * TY] = wide.astype(BF16)
        goals.append(wide[V : V + 8])
    wide = jnp.transpose(ext[...])
    prof[:, ROWS * TY : Q] = wide.astype(BF16)
    goal = wide_of(goals[1 : ROWS - 1] + [wide[V : V + 8]])
    goal = goal + jnp.concatenate([goal[3:8], goal[0:3]], axis=0)

    width = NA * TY
    lane = iota((8, width), 1)
    main = lane < (NA - 1) * TY
    spot = lane - (NA - 1) * TY
    row_at = jnp.where(main, lane // TY + 1, spot // 8)
    grid_x = patch * TX + row_at - TX
    inside_x = (grid_x >= 0) & (grid_x < lax.axis_size("patch") * TX)
    low = (spot % 8 == 3) & (body > 0)
    high = (spot % 8 == 2) & (body < lax.axis_size("body") - 1)
    ring = main | ((row_at >= 1) & (row_at <= ROWS - 2) & (low | high))
    mask = (ring & inside_x & (iota((8, width), 0) < 3)).astype(F32)

    def fill(zs_at, zb_at, p):
        for n in range(2):
            u1 = dot(wa[2 * p + n], prof[...])
            z1 = (u1 + u1 * jnp.tanh(u1)).astype(BF16)
            for r in range(TX):
                u1s[2 * p + n, r] = u1[:, (TX + r) * TY : (TX + r + 1) * TY]
            beside = z1[:, ROWS * TY : Q]
            for row in range(ROWS):
                for m, part in enumerate(three(z1[:, row * TY : (row + 1) * TY], beside, row)):
                    at = (3 * row + m) * C
                    zs_at[n, at : at + C, :] = part
            for tap, shift in enumerate(BESIDE):
                zb_at[n, tap * C : (tap + 1) * C, :] = turned(beside, shift)

    def wall(zs_at, zb_at, p):
        spots = [(n, t) for n in range(2) for t in range(NA)]

        def taps(n, t):
            return zb_at[n] if t == NA - 1 else zs_at[n, 3 * C * t : 3 * C * t + KB, :]

        for g in range(0, 2 * NA, 2):
            pair = spots[g : g + 2]
            both = dot(wf[...], wide_of([taps(n, t) for n, t in pair]))
            for m, (n, t) in enumerate(pair):
                u2 = both[:, TY * m : TY * (m + 1)]
                u2s[2 * p + n, t] = u2
                z1 = taps(n, t)[4 * C : 5 * C].astype(F32)
                act = z1 + (u2 + u2 * jnp.tanh(u2))
                rows = pl.ds(pl.multiple_of((2 * p + n) * C, C), C)
                z2s[t, rows, :] = act.astype(BF16)

    def forward(p, _):
        zs_at = zs.at[pl.ds(2 * p, 4)]
        zb_at = zb.at[pl.ds(2 * p, 4)]
        fill(zs_at.at[2:4], zb_at.at[2:4], p + 1)
        wall(zs_at.at[0:2], zb_at.at[0:2], p)
        return 0

    fill(zs.at[0:2], zb.at[0:2], 0)
    lax.fori_loop(0, H // 2 - 1, forward, 0)
    wall(zs.at[H - 2 : H], zb.at[H - 2 : H], H // 2 - 1)
    stress = wide_of(
        [dot(wh[...], wide_of([z2s[t] for t in range(n, min(n + 2, NA))])) for n in range(0, NA, 2)]
    )
    for r in range(TX):
        stress_out[:, r, :] = stress[0:3, (1 + r) * TY : (2 + r) * TY]
    err = ((stress - goal) * mask).astype(BF16)
    err_s[...] = err
    grad_h = dot_t(err[:, TY : 3 * TY], wide_of([z2s[1], z2s[2]]))
    for t in range(H * C // 128):
        grads[108 + t] = grad_h[:, t * 128 : (t + 1) * 128]
    unf[...] = dot(sel[...], prof[:, TX * TY : 2 * TX * TY]).astype(BF16).reshape(H, 16, TX * TY)
    gb[...] = jnp.zeros_like(gb)

    def third(das_at, dz_at, p):
        mids = []
        kept = []
        for n in range(2):
            h = 2 * p + n
            u2 = wide_of([u2s[h, t] for t in range(NA)])
            t2 = jnp.tanh(u2)
            dz2 = dot(wht[h], err_s[...])
            da2 = (dz2 * ((1.0 + t2) * (1.0 + u2 * (1.0 - t2)))).astype(BF16)
            beside = da2[:, (NA - 1) * TY : width]
            for t in range(NA - 1):
                for m, part in enumerate(three(da2[:, t * TY : (t + 1) * TY], beside, t + 1)):
                    at = (3 * t + m) * C
                    das_at[n, at : at + C, :] = part
            dz_at[n] = dz2[:, TY : 3 * TY]
            mids.append(da2[:, TY : 3 * TY])
            kept += [zs[h, 3 * C * t : 3 * C * t + KB, :] for t in (1, 2)]
        gb[...] += dot_t(wide_of(mids), wide_of(kept))

    def fourth(das_at, dz_at, p, grad_a):
        for n in range(2):
            h = 2 * p + n
            conv = dot(wb[...], wide_of([das_at[n, 3 * C * t : 3 * C * t + KB, :] for t in range(TX)]))
            u1 = wide_of([u1s[h, r] for r in range(TX)])
            t1 = jnp.tanh(u1)
            da1 = ((dz_at[n] + conv) * ((1.0 + t1) * (1.0 + u1 * (1.0 - t1)))).astype(BF16)
            rows = pl.ds(pl.multiple_of(h * C, C), C)
            for r in range(TX):
                da1s[r, rows, :] = da1[:, r * TY : (r + 1) * TY]
            grad_a = grad_a + dot_t(unf[h], da1)
        return grad_a

    def backward(p, grad_a):
        das_at = das.at[pl.ds(2 * p, 4)]
        dz_at = dzs.at[pl.ds(2 * p, 4)]
        third(das_at.at[2:4], dz_at.at[2:4], p + 1)
        return fourth(das_at.at[0:2], dz_at.at[0:2], p, grad_a)

    third(das.at[0:2], dzs.at[0:2], 0)
    grad_a = lax.fori_loop(0, H // 2 - 1, backward, jnp.zeros((16, C), F32))
    grad_a = fourth(das.at[H - 2 : H], dzs.at[H - 2 : H], H // 2 - 1, grad_a)
    blank = jnp.zeros((16, 128 - C), F32)
    grad_a = jnp.concatenate([grad_a, blank], axis=1)
    grads[126] = grad_a[0:8]
    grads[127] = grad_a[8:16]
    grad_b = jnp.transpose(gb[...])
    blank = jnp.zeros((KB, 128 - C), F32)
    grads[0:108] = jnp.concatenate([grad_b, blank], axis=1).reshape(108, 8, 128)
    back = dot(wat[...], wide_of([da1s[r] for r in range(TX)]))
    for r in range(TX):
        pgrad[:, r, :] = back[0:V, r * TY : (r + 1) * TY]


def spread_kernel(sums, grad_a, grad_b, grad_h):
    for tap in range(9):
        rows = sums[12 * tap : 12 * (tap + 1)].astype(F32).reshape(C, 128)
        grad_b[tap] = rows[:, 0:C]
    for t in range(H * C // 128):
        grad_h[:, t * 128 : (t + 1) * 128] = sums[108 + t].astype(F32)[0:3]
    low = sums[126].astype(F32)[:, 0:C]
    high = sums[127].astype(F32)[:, 0:C]
    for k in range(3):
        for f in range(F):
            n = k * F + f
            grad_a[f, k : k + 1, :] = low[n : n + 1] if n < 8 else high[n - 8 : n - 7]


def call(kernel, limit, out_shape, scratch=(), space=pltpu.VMEM):
    near = pl.BlockSpec(memory_space=pltpu.VMEM)

    def run(*operands):
        return pl.pallas_call(
            kernel,
            out_shape=out_shape,
            in_specs=[pl.BlockSpec(memory_space=space)] * len(operands),
            out_specs=jax.tree.map(lambda _: near, out_shape),
            scratch_shapes=list(scratch),
            compiler_params=pltpu.CompilerParams(vmem_limit_bytes=limit * MIB),
        )(*operands)

    return run


def shape(dims, kind):
    return jax.ShapeDtypeStruct(dims, kind)


def exchange(blocks):
    return lax.all_to_all(blocks, AXES, split_axis=0, concat_axis=0, tiled=True)


def trades(count):
    inner = [(i, i ^ 1) for i in range(count)]
    outer = [(i, i - 1 + 2 * (i % 2)) for i in range(1, count - 1)] + [(0, 0), (count - 1, count - 1)]
    return inner, outer


def shards(donors, owner, slot, target, weight_a, weight_b, weight_h):
    n_patch = lax.axis_size("patch")
    n_body = lax.axis_size("body")
    n_dev = n_patch * n_body
    rows = donors.shape[1]
    cap = 2 * rows // n_dev
    outbox = call(
        functools.partial(pack_kernel, cap),
        12,
        shape((n_dev * cap, 128), BF16),
        [
            pltpu.VMEM((128, rows), BF16),
            pltpu.VMEM((1, rows), jnp.int32),
            pltpu.VMEM((1, rows), jnp.int32),
            pltpu.VMEM((rows, n_dev), F32),
            pltpu.SemaphoreType.DMA((3,)),
        ],
        pltpu.HBM,
    )(donors, owner.reshape(1, rows), slot.reshape(1, rows))
    inbox = exchange(outbox.reshape(n_dev, cap, 128)).reshape(n_dev * cap, 128)

    half = jnp.asarray(0.5, BF16)
    heights = jnp.arange(H)
    reach = heights[None, :, None] + 2 * (jnp.arange(3)[:, None, None] - 1) == heights[None, None, :]
    band = jnp.einsum("khg,kfc->hcgf", reach.astype(BF16), weight_a).reshape(H * C, V)
    band = jnp.pad(band, ((0, 0), (0, 128 - V)))
    wa = (band * half).reshape(H, C, 128)
    wat = jnp.transpose(band)
    wf = jnp.transpose(weight_b, (2, 0, 1)).reshape(C, KB) * half
    wb = jnp.transpose(weight_b[::-1], (1, 0, 2)).reshape(C, KB) * half
    wh = jnp.pad(jnp.transpose(weight_h), ((0, 5), (0, 0)))
    wht = (jnp.pad(weight_h, ((0, 0), (0, 5))) * half).reshape(H, C, 8)
    line = jnp.arange(16)
    want = (heights[:, None] + 2 * (line[None, :] // F - 1)) * F + line[None, :] % F
    sel = (want[:, :, None] == jnp.arange(128)[None, None, :]) & (want >= 0)[:, :, None]
    sel = sel & (want < V)[:, :, None] & (line < 15)[None, :, None]
    sel = sel.astype(BF16).reshape(H * 16, 128)

    inbox, wa, wat, wf, wb, wh, wht, sel = lax.optimization_barrier(
        (inbox, wa, wat, wf, wb, wh, wht, sel)
    )
    prof, left, right = call(
        unpack_kernel,
        8,
        (shape((TX * TY, 128), BF16), shape((16, 128), BF16), shape((16, 128), BF16)),
        [pltpu.VMEM((128, 128), F32)],
    )(inbox, jnp.transpose(target, (2, 0, 1)))
    edges = jnp.concatenate([left, right], axis=0)
    sides = [lax.ppermute(edges, "body", trade) for trade in trades(n_body)]
    tile = jnp.concatenate([prof] + sides, axis=0)
    first, second = [lax.ppermute(tile, "patch", trade) for trade in trades(n_patch)]

    stress, pgrad, grads = call(
        step_kernel,
        46,
        (shape((3, TX, TY), F32), shape((V, TX, TY), F32), shape((128, 8, 128), F32)),
        [
            pltpu.VMEM((128, 128), F32),
            pltpu.VMEM((128, Q), BF16),
            pltpu.VMEM((H, 16, TX * TY), BF16),
            pltpu.VMEM((H, 3 * ROWS * C, TY), BF16),
            pltpu.VMEM((H, KB, TY), BF16),
            pltpu.VMEM((H, TX, C, TY), F32),
            pltpu.VMEM((H, NA, C, TY), F32),
            pltpu.VMEM((NA, H * C, TY), BF16),
            pltpu.VMEM((H, 3 * (NA - 1) * C, TY), BF16),
            pltpu.VMEM((H, C, TX * TY), F32),
            pltpu.VMEM((TX, H * C, TY), BF16),
            pltpu.VMEM((8, NA * TY), BF16),
            pltpu.VMEM((C, KB), F32),
        ],
    )(tile, first, second, wa, wat, wf, wb, wh, wht, sel)
    scale = 1.0 / jnp.sqrt(jnp.float32(TX * TY * n_dev))
    total = (jnp.sum(exchange(grads), axis=0) * scale).astype(BF16)
    sums = exchange(jnp.broadcast_to(total[None], (n_dev, 8, 128)))
    grad_a, grad_b, grad_h = call(
        spread_kernel,
        6,
        (shape((F, 3, C), F32), shape((9, C, C), F32), shape((3, H * C), F32)),
    )(sums)
    return (
        jnp.transpose(stress, (1, 2, 0)),
        pgrad,
        jnp.transpose(grad_a, (1, 0, 2)),
        grad_b,
        jnp.transpose(grad_h),
    )


def solution(mesh):
    placed = (
        P(None, ("patch", "body")),
        P(("patch", "body"), None),
        P(("patch", "body")),
        P("patch", "body", None),
        P(),
        P(),
        P(),
    )
    return jax.shard_map(
        shards,
        mesh=mesh,
        in_specs=placed,
        out_specs=(P("patch", "body", None), P(None, "patch", "body"), P(), P(), P()),
        check_vma=False,
    )
```

```python
import functools

import jax
import jax.numpy as jnp
from jax import lax
from jax.experimental import pallas as pl
from jax.experimental.pallas import tpu as pltpu
from jax.sharding import PartitionSpec as P

F32 = jnp.float32
BF16 = jnp.bfloat16
AXES = ("patch", "body")
C = 96
H = 24
F = 5
V = H * F
TX = 2
TY = 128
ROWS = TX + 4
NZ = ROWS + 1
NA = ROWS - 1
Q = NZ * TY
KB = 9 * C
BESIDE = tuple((di - 1) * 8 + (dj - 1) * 2 for di in range(3) for dj in range(3))
COLS = (((1,), (1,)), ((), ()))
MIB = 1024 * 1024
FORWARD = (("F", 0), ("W", 0), ("F", 1), ("W", 1), ("W", 2), ("W", 3), ("W", 4))
BACKWARD = (("T", 0), ("B", 0), ("T", 1), ("G", 0), ("B", 1))


def dot(a, b):
    return jnp.dot(a, b, preferred_element_type=F32)


def dot_t(a, b):
    return lax.dot_general(a, b, COLS, preferred_element_type=F32)


def iota(shape, dim):
    return lax.broadcasted_iota(jnp.int32, shape, dim)


def pack_kernel(cap, donors_far, owner_far, slot_far, out, dext, owner, slot, ranked, place, box, sems):
    rows = donors_far.shape[1]
    n_dev = 128
    own_copy = pltpu.make_async_copy(owner_far, owner, sems.at[0])
    slot_copy = pltpu.make_async_copy(slot_far, slot, sems.at[1])
    donor_copy = pltpu.make_async_copy(donors_far, dext.at[0:V], sems.at[2])
    own_copy.start()
    slot_copy.start()
    donor_copy.start()
    part = 256
    upper = (iota((part, part), 0) < iota((part, part), 1)).astype(F32).astype(BF16)
    own_copy.wait()

    def count(n, carry):
        dest = owner[:, pl.ds(pl.multiple_of(n * part, part), part)]
        hit = (iota((n_dev, part), 0) == dest).astype(F32)
        before = dot(hit.astype(BF16), upper) + carry
        rank = jnp.sum(before * hit, axis=0, keepdims=True)
        spot = (dest * cap).astype(F32) + rank
        ranked[2 * n] = spot[:, 0:128]
        ranked[2 * n + 1] = spot[:, 128:256]
        return carry + jnp.sum(hit, axis=1, keepdims=True)

    lax.fori_loop(0, rows // part, count, jnp.zeros((n_dev, 1), F32))
    block = 256
    tall = jnp.transpose(jnp.concatenate([ranked[n] for n in range(rows // 128)], axis=0))
    for n in range(rows // 128):
        place[n * 128 : (n + 1) * 128, :] = jnp.broadcast_to(tall[:, n : n + 1], (128, 128))
    slot_copy.wait()
    pad = iota((8, rows), 0)
    dext[V : V + 8, :] = jnp.where(pad == 0, slot[...], 0).astype(F32).astype(BF16)
    donor_copy.wait()
    marks = [(iota((1, 128), 1) + 128 * t).astype(F32) for t in range(2)]
    one, none = jnp.asarray(1.0, BF16), jnp.asarray(0.0, BF16)

    def boxed(n):
        at = pl.ds(pl.multiple_of(n * 4 * block, 4 * block), 4 * block)
        return pltpu.make_async_copy(box.at[at], out.at[at], sems.at[3 + n])

    def step(n, _):
        for m in range(4):
            base = ((4 * n + m) * block).astype(F32)
            spots = place[...]
            pick = jnp.concatenate([jnp.where(spots == mark + base, one, none) for mark in marks], axis=1)
            picked = dot(dext[...], pick)
            at = pl.ds(pl.multiple_of((4 * n + m) * block, block), block)
            box[at, :] = jnp.transpose(picked).astype(BF16)
        boxed(n).start()
        return 0

    steps = n_dev * cap // block // 4
    lax.fori_loop(0, steps, step, 0)
    for n in range(steps):
        boxed(n).wait()


def unpack_kernel(inbox, target, prof, left, right, side):
    total = inbox.shape[0]
    points = TX * TY
    lane = iota((8, 128), 1)
    mark = (lane == V).astype(F32).astype(BF16)
    acc = jnp.zeros((points, 128), F32)
    chunk = 1024
    for at in range(0, total, chunk):
        rows = inbox[at : at + chunk, :]
        slots = dot_t(mark, rows)[0:1, :].astype(jnp.int32)
        pick = (iota((points, chunk), 0) == slots).astype(F32).astype(BF16)
        acc = acc + dot(pick, rows)
    acc = jnp.where(iota((points, 128), 1) < V, acc, 0.0)
    for r in range(TX):
        goal = target[:, r, :]
        high = goal.astype(BF16).astype(F32)
        rest = goal - high
        side[...] = jnp.zeros((128, 128), F32)
        side[V : V + 3, :] = high
        side[V + 3 : V + 6, :] = rest
        part = acc[r * TY : (r + 1) * TY, :] + jnp.transpose(side[...])
        prof[r * TY : (r + 1) * TY, :] = part.astype(BF16)
        if r == 0:
            keep = part
    side[0:2, :] = keep[0:2, :]
    side[2:4, :] = part[0:2, :]
    side[4:16, :] = jnp.zeros((12, 128), F32)
    left[...] = side[0:16, :].astype(BF16)
    side[0:2, :] = keep[TY - 2 : TY, :]
    side[2:4, :] = part[TY - 2 : TY, :]
    right[...] = side[0:16, :].astype(BF16)


def turned(tile, shift):
    return tile if shift == 0 else pltpu.roll(tile, (-shift) % TY, 1)


def three(tile, beside, row):
    ends = turned(beside, 8 * row + 3)
    lane = iota((C, TY), 1)
    return (
        jnp.where(lane == 0, ends, turned(tile, -1)),
        tile,
        jnp.where(lane == TY - 1, ends, turned(tile, 1)),
    )


def wide_of(tiles):
    return jnp.concatenate(list(tiles), axis=1)


def step_kernel(own, first, second, wa, wat, wf, wb, wh, wht, sel, stress_out, pgrad, grads,
                ext, prof, unf, zs, zb, u1s, u2s, z2s, das, dzs, da1s, err_s, gb):
    patch = lax.axis_index("patch")
    body = lax.axis_index("body")
    odd_x = patch % 2 == 1
    odd_y = body % 2 == 1
    has_left = jnp.where(body > 0, 1.0, 0.0)
    has_right = jnp.where(body < lax.axis_size("body") - 1, 1.0, 0.0)
    has_up = jnp.where(patch > 0, 1.0, 0.0)
    has_down = jnp.where(patch < lax.axis_size("patch") - 1, 1.0, 0.0)
    ext[...] = jnp.zeros((128, 128), F32)
    goals = []
    one, two = first[...].astype(F32), second[...].astype(F32)
    sources = (
        jnp.where(odd_x, one, two) * has_up,
        own[...].astype(F32),
        jnp.where(odd_x, two, one) * has_down,
    )
    for row in range(ROWS):
        src, r = sources[row // TX], row % TX
        block = src[r * TY : (r + 1) * TY, :]
        one, two = src[256:288], src[288:320]
        left = jnp.where(odd_y, one, two)[16 + 2 * r : 18 + 2 * r] * has_left
        right = jnp.where(odd_y, two, one)[2 * r : 2 * r + 2] * has_right
        parts = (block[TY - 1 : TY], left[0:1], right[0:1], left[1:2], right[1:2], block[0:1])
        for n, part in enumerate(parts):
            ext[8 * row + n : 8 * row + n + 1, :] = part
        wide = jnp.transpose(block)
        prof[:, row * TY : (row + 1) * TY] = wide.astype(BF16)
        goals.append(wide[V : V + 8])
    wide = jnp.transpose(ext[...])
    prof[:, ROWS * TY : Q] = wide.astype(BF16)
    goal = wide_of(goals[1 : ROWS - 1] + [wide[V : V + 8]])
    goal = goal + jnp.concatenate([goal[3:8], goal[0:3]], axis=0)

    width = NA * TY
    lane = iota((8, width), 1)
    main = lane < (NA - 1) * TY
    spot = lane - (NA - 1) * TY
    row_at = jnp.where(main, lane // TY + 1, spot // 8)
    grid_x = patch * TX + row_at - TX
    inside_x = (grid_x >= 0) & (grid_x < lax.axis_size("patch") * TX)
    low = (spot % 8 == 3) & (body > 0)
    high = (spot % 8 == 2) & (body < lax.axis_size("body") - 1)
    ring = main | ((row_at >= 1) & (row_at <= ROWS - 2) & (low | high))
    mask = (ring & inside_x & (iota((8, width), 0) < 3)).astype(F32)

    def fill(zs_at, zb_at, p, which=(0, 1)):
        for n in which:
            u1 = dot(wa[2 * p + n], prof[...])
            z1 = (u1 + u1 * jnp.tanh(u1)).astype(BF16)
            for r in range(TX):
                u1s[2 * p + n, r] = u1[:, (TX + r) * TY : (TX + r + 1) * TY]
            beside = z1[:, ROWS * TY : Q]
            for row in range(ROWS):
                for m, part in enumerate(three(z1[:, row * TY : (row + 1) * TY], beside, row)):
                    at = (3 * row + m) * C
                    zs_at[n, at : at + C, :] = part
            for tap, shift in enumerate(BESIDE):
                zb_at[n, tap * C : (tap + 1) * C, :] = turned(beside, shift)

    def wall(zs_at, zb_at, p, which=range(NA)):
        spots = [(n, t) for n in range(2) for t in range(NA)]

        def taps(n, t):
            return zb_at[n] if t == NA - 1 else zs_at[n, 3 * C * t : 3 * C * t + KB, :]

        for g in which:
            pair = spots[2 * g : 2 * g + 2]
            both = dot(wf[...], wide_of([taps(n, t) for n, t in pair]))
            for m, (n, t) in enumerate(pair):
                u2 = both[:, TY * m : TY * (m + 1)]
                u2s[2 * p + n, t] = u2
                z1 = taps(n, t)[4 * C : 5 * C].astype(F32)
                act = z1 + (u2 + u2 * jnp.tanh(u2))
                rows = pl.ds(pl.multiple_of((2 * p + n) * C, C), C)
                z2s[t, rows, :] = act.astype(BF16)

    def forward(zs_at, zb_at, p):
        for kind, n in FORWARD:
            if kind == "F":
                fill(zs_at.at[2:4], zb_at.at[2:4], p + 1, (n,))
            else:
                wall(zs_at.at[0:2], zb_at.at[0:2], p, (n,))

    def forward_two(q, _):
        zs_at = zs.at[pl.ds(4 * q + 2, 6)]
        zb_at = zb.at[pl.ds(4 * q + 2, 6)]
        for m in range(2):
            at = slice(2 * m, 2 * m + 4)
            forward(zs_at.at[at], zb_at.at[at], 2 * q + 1 + m)
        return 0

    fill(zs.at[0:2], zb.at[0:2], 0)
    forward(zs.at[0:4], zb.at[0:4], 0)
    lax.fori_loop(0, H // 4 - 1, forward_two, 0)
    wall(zs.at[H - 2 : H], zb.at[H - 2 : H], H // 2 - 1)
    stress = wide_of(
        [dot(wh[...], wide_of([z2s[t] for t in range(n, min(n + 2, NA))])) for n in range(0, NA, 2)]
    )
    for r in range(TX):
        stress_out[:, r, :] = stress[0:3, (1 + r) * TY : (2 + r) * TY]
    err = ((stress - goal) * mask).astype(BF16)
    err_s[...] = err
    grad_h = dot_t(err[:, TY : 3 * TY], wide_of([z2s[1], z2s[2]]))
    for t in range(H * C // 128):
        grads[108 + t] = grad_h[:, t * 128 : (t + 1) * 128]
    unf[...] = dot(sel[...], prof[:, TX * TY : 2 * TX * TY]).astype(BF16).reshape(H, 16, TX * TY)
    gb[...] = jnp.zeros_like(gb)

    def third(das_at, dz_at, p, which=(0, 1)):
        for n in which:
            h = 2 * p + n
            u2 = wide_of([u2s[h, t] for t in range(NA)])
            t2 = jnp.tanh(u2)
            dz2 = dot(wht[h], err_s[...])
            da2 = (dz2 * ((1.0 + t2) * (1.0 + u2 * (1.0 - t2)))).astype(BF16)
            beside = da2[:, (NA - 1) * TY : width]
            for t in range(NA - 1):
                for m, part in enumerate(three(da2[:, t * TY : (t + 1) * TY], beside, t + 1)):
                    at = (3 * t + m) * C
                    das_at[n, at : at + C, :] = part
            dz_at[n] = dz2[:, TY : 3 * TY]

    def fifth(das_at, p):
        spots = [(n, t) for n in range(2) for t in (1, 2)]
        mids = [das_at[n, (3 * t + 1) * C : (3 * t + 2) * C, :] for n, t in spots]
        kept = [zs[2 * p + n, 3 * C * t : 3 * C * t + KB, :] for n, t in spots]
        gb[...] += dot_t(wide_of(mids), wide_of(kept))

    def fourth(das_at, dz_at, p, grad_a, which=(0, 1)):
        for n in which:
            h = 2 * p + n
            conv = dot(wb[...], wide_of([das_at[n, 3 * C * t : 3 * C * t + KB, :] for t in range(TX)]))
            u1 = wide_of([u1s[h, r] for r in range(TX)])
            t1 = jnp.tanh(u1)
            da1 = ((dz_at[n] + conv) * ((1.0 + t1) * (1.0 + u1 * (1.0 - t1)))).astype(BF16)
            rows = pl.ds(pl.multiple_of(h * C, C), C)
            for r in range(TX):
                da1s[r, rows, :] = da1[:, r * TY : (r + 1) * TY]
            grad_a = grad_a + dot_t(unf[h], da1)
        return grad_a

    def backward(das_at, dz_at, p, grad_a):
        for kind, n in BACKWARD:
            if kind == "T":
                third(das_at.at[2:4], dz_at.at[2:4], p + 1, (n,))
            elif kind == "G":
                fifth(das_at.at[0:2], p)
            else:
                grad_a = fourth(das_at.at[0:2], dz_at.at[0:2], p, grad_a, (n,))
        return grad_a

    def backward_two(q, grad_a):
        das_at = das.at[pl.ds(4 * q + 2, 6)]
        dz_at = dzs.at[pl.ds(4 * q + 2, 6)]
        for m in range(2):
            at = slice(2 * m, 2 * m + 4)
            grad_a = backward(das_at.at[at], dz_at.at[at], 2 * q + 1 + m, grad_a)
        return grad_a

    third(das.at[0:2], dzs.at[0:2], 0)
    grad_a = backward(das.at[0:4], dzs.at[0:4], 0, jnp.zeros((16, C), F32))
    grad_a = lax.fori_loop(0, H // 4 - 1, backward_two, grad_a)
    fifth(das.at[H - 2 : H], H // 2 - 1)
    grad_a = fourth(das.at[H - 2 : H], dzs.at[H - 2 : H], H // 2 - 1, grad_a)
    blank = jnp.zeros((16, 128 - C), F32)
    grad_a = jnp.concatenate([grad_a, blank], axis=1)
    grads[126] = grad_a[0:8]
    grads[127] = grad_a[8:16]
    grad_b = jnp.transpose(gb[...])
    blank = jnp.zeros((KB, 128 - C), F32)
    grads[0:108] = jnp.concatenate([grad_b, blank], axis=1).reshape(108, 8, 128)
    back = dot(wat[...], wide_of([da1s[r] for r in range(TX)]))
    for r in range(TX):
        pgrad[:, r, :] = back[0:V, r * TY : (r + 1) * TY]


def spread_kernel(sums, grad_a, grad_b, grad_h):
    for tap in range(9):
        rows = sums[12 * tap : 12 * (tap + 1)].astype(F32).reshape(C, 128)
        grad_b[tap] = rows[:, 0:C]
    for t in range(H * C // 128):
        grad_h[:, t * 128 : (t + 1) * 128] = sums[108 + t].astype(F32)[0:3]
    low = sums[126].astype(F32)[:, 0:C]
    high = sums[127].astype(F32)[:, 0:C]
    for k in range(3):
        for f in range(F):
            n = k * F + f
            grad_a[f, k : k + 1, :] = low[n : n + 1] if n < 8 else high[n - 8 : n - 7]


def call(kernel, limit, out_shape, scratch=(), space=pltpu.VMEM, flags=None):
    near = pl.BlockSpec(memory_space=space)

    def run(*operands):
        return pl.pallas_call(
            kernel,
            out_shape=out_shape,
            in_specs=[near] * len(operands),
            out_specs=jax.tree.map(lambda _: near, out_shape),
            scratch_shapes=list(scratch),
            compiler_params=pltpu.CompilerParams(vmem_limit_bytes=limit * MIB, flags=flags),
        )(*operands)

    return run


def shape(dims, kind):
    return jax.ShapeDtypeStruct(dims, kind)


def exchange(blocks):
    return lax.all_to_all(blocks, AXES, split_axis=0, concat_axis=0, tiled=True)


def trades(count):
    inner = [(i, i ^ 1) for i in range(count)]
    outer = [(i, i - 1 + 2 * (i % 2)) for i in range(1, count - 1)] + [(0, 0), (count - 1, count - 1)]
    return inner, outer


def shards(donors, owner, slot, target, weight_a, weight_b, weight_h):
    n_patch = lax.axis_size("patch")
    n_body = lax.axis_size("body")
    n_dev = n_patch * n_body
    rows = donors.shape[1]
    cap = 2 * rows // n_dev
    outbox = call(
        functools.partial(pack_kernel, cap),
        60,
        shape((n_dev * cap, 128), BF16),
        [
            pltpu.VMEM((128, rows), BF16),
            pltpu.VMEM((1, rows), jnp.int32),
            pltpu.VMEM((1, rows), jnp.int32),
            pltpu.VMEM((rows // 128, 1, 128), F32),
            pltpu.VMEM((rows, 128), F32),
            pltpu.VMEM((n_dev * cap, 128), BF16),
            pltpu.SemaphoreType.DMA((3 + n_dev * cap // 1024,)),
        ],
        pltpu.HBM,
    )(donors, owner.reshape(1, rows), slot.reshape(1, rows))
    inbox = exchange(outbox.reshape(n_dev, cap, 128)).reshape(n_dev * cap, 128)

    half = jnp.asarray(0.5, BF16)
    heights = jnp.arange(H)
    reach = heights[None, :, None] + 2 * (jnp.arange(3)[:, None, None] - 1) == heights[None, None, :]
    band = jnp.einsum("khg,kfc->hcgf", reach.astype(BF16), weight_a).reshape(H * C, V)
    band = jnp.pad(band, ((0, 0), (0, 128 - V)))
    wa = (band * half).reshape(H, C, 128)
    wat = jnp.transpose(band)
    wf = jnp.transpose(weight_b, (2, 0, 1)).reshape(C, KB) * half
    wb = jnp.transpose(weight_b[::-1], (1, 0, 2)).reshape(C, KB) * half
    wh = jnp.pad(jnp.transpose(weight_h), ((0, 5), (0, 0)))
    wht = (jnp.pad(weight_h, ((0, 0), (0, 5))) * half).reshape(H, C, 8)
    line = jnp.arange(16)
    want = (heights[:, None] + 2 * (line[None, :] // F - 1)) * F + line[None, :] % F
    sel = (want[:, :, None] == jnp.arange(128)[None, None, :]) & (want >= 0)[:, :, None]
    sel = sel & (want < V)[:, :, None] & (line < 15)[None, :, None]
    sel = sel.astype(BF16).reshape(H * 16, 128)

    inbox, wa, wat, wf, wb, wh, wht, sel = lax.optimization_barrier(
        (inbox, wa, wat, wf, wb, wh, wht, sel)
    )
    prof, left, right = call(
        unpack_kernel,
        8,
        (shape((TX * TY, 128), BF16), shape((16, 128), BF16), shape((16, 128), BF16)),
        [pltpu.VMEM((128, 128), F32)],
    )(inbox, jnp.transpose(target, (2, 0, 1)))
    edges = jnp.concatenate([left, right], axis=0)
    sides = [lax.ppermute(edges, "body", trade) for trade in trades(n_body)]
    tile = jnp.concatenate([prof] + sides, axis=0)
    first, second = [lax.ppermute(tile, "patch", trade) for trade in trades(n_patch)]

    stress, pgrad, grads = call(
        step_kernel,
        46,
        (shape((3, TX, TY), F32), shape((V, TX, TY), F32), shape((128, 8, 128), F32)),
        [
            pltpu.VMEM((128, 128), F32),
            pltpu.VMEM((128, Q), BF16),
            pltpu.VMEM((H, 16, TX * TY), BF16),
            pltpu.VMEM((H, 3 * ROWS * C, TY), BF16),
            pltpu.VMEM((H, KB, TY), BF16),
            pltpu.VMEM((H, TX, C, TY), F32),
            pltpu.VMEM((H, NA, C, TY), F32),
            pltpu.VMEM((NA, H * C, TY), BF16),
            pltpu.VMEM((H, 3 * (NA - 1) * C, TY), BF16),
            pltpu.VMEM((H, C, TX * TY), F32),
            pltpu.VMEM((TX, H * C, TY), BF16),
            pltpu.VMEM((8, NA * TY), BF16),
            pltpu.VMEM((C, KB), F32),
        ],
    )(tile, first, second, wa, wat, wf, wb, wh, wht, sel)
    scale = 1.0 / jnp.sqrt(jnp.float32(TX * TY * n_dev))
    total = (jnp.sum(exchange(grads), axis=0) * scale).astype(BF16)
    sums = exchange(jnp.broadcast_to(total[None], (n_dev, 8, 128)))
    grad_a, grad_b, grad_h = call(
        spread_kernel,
        6,
        (shape((F, 3, C), F32), shape((9, C, C), F32), shape((3, H * C), F32)),
    )(sums)
    return (
        jnp.transpose(stress, (1, 2, 0)),
        pgrad,
        jnp.transpose(grad_a, (1, 0, 2)),
        grad_b,
        jnp.transpose(grad_h),
    )


def solution(mesh):
    placed = (
        P(None, ("patch", "body")),
        P(("patch", "body"), None),
        P(("patch", "body")),
        P("patch", "body", None),
        P(),
        P(),
        P(),
    )
    return jax.shard_map(
        shards,
        mesh=mesh,
        in_specs=placed,
        out_specs=(P("patch", "body", None), P(None, "patch", "body"), P(), P(), P()),
        check_vma=False,
    )
```

```python
import functools

import jax
import jax.numpy as jnp
from jax import lax
from jax.experimental import pallas as pl
from jax.experimental.pallas import tpu as pltpu
from jax.sharding import PartitionSpec as P

F32 = jnp.float32
BF16 = jnp.bfloat16
AXES = ("patch", "body")
C = 96
H = 24
F = 5
V = H * F
TX = 2
TY = 128
ROWS = TX + 4
NZ = ROWS + 1
NA = ROWS - 1
Q = NZ * TY
KB = 9 * C
BESIDE = tuple((di - 1) * 8 + (dj - 1) * 2 for di in range(3) for dj in range(3))
KT = -(-KB // 128)
GH = 3 * H * C // 128
SMALL = 768 - KT * C
COLS = (((1,), (1,)), ((), ()))
MIB = 1024 * 1024
TRIP = 5
FORWARD = (("F", 0), ("W", 0), ("F", 1), ("W", 1), ("W", 2), ("W", 3), ("W", 4))
BACKWARD = (("T", 0), ("B", 0), ("T", 1), ("G", 0), ("B", 1))


def dot(a, b):
    return jnp.dot(a, b, preferred_element_type=F32)


def dot_t(a, b):
    return lax.dot_general(a, b, COLS, preferred_element_type=F32)


def iota(shape, dim):
    return lax.broadcasted_iota(jnp.int32, shape, dim)


def pack_kernel(cap, donors_far, owner_far, slot_far, out, dext, owner, slot, ranked, place, box, sems):
    rows = donors_far.shape[1]
    n_dev = 128
    own_copy = pltpu.make_async_copy(owner_far, owner, sems.at[0])
    slot_copy = pltpu.make_async_copy(slot_far, slot, sems.at[1])
    donor_copy = pltpu.make_async_copy(donors_far, dext.at[0:V], sems.at[2])
    own_copy.start()
    slot_copy.start()
    donor_copy.start()
    part = 256
    upper = (iota((part, part), 0) < iota((part, part), 1)).astype(F32).astype(BF16)
    own_copy.wait()

    def count(n, carry):
        dest = owner[:, pl.ds(pl.multiple_of(n * part, part), part)]
        hit = (iota((n_dev, part), 0) == dest).astype(F32)
        before = dot(hit.astype(BF16), upper) + carry
        rank = jnp.sum(before * hit, axis=0, keepdims=True)
        spot = (dest * cap).astype(F32) + rank
        ranked[2 * n] = spot[:, 0:128]
        ranked[2 * n + 1] = spot[:, 128:256]
        return carry + jnp.sum(hit, axis=1, keepdims=True)

    lax.fori_loop(0, rows // part, count, jnp.zeros((n_dev, 1), F32))
    block = 256
    tall = jnp.transpose(jnp.concatenate([ranked[n] for n in range(rows // 128)], axis=0))
    for n in range(rows // 128):
        place[n * 128 : (n + 1) * 128, :] = jnp.broadcast_to(tall[:, n : n + 1], (128, 128))
    slot_copy.wait()
    pad = iota((8, rows), 0)
    dext[V : V + 8, :] = jnp.where(pad == 0, slot[...], 0).astype(F32).astype(BF16)
    donor_copy.wait()
    marks = [(iota((1, 128), 1) + 128 * t).astype(F32) for t in range(2)]
    one, none = jnp.asarray(1.0, BF16), jnp.asarray(0.0, BF16)

    def boxed(n):
        at = pl.ds(pl.multiple_of(n * 4 * block, 4 * block), 4 * block)
        return pltpu.make_async_copy(box.at[at], out.at[at], sems.at[3 + n])

    def step(n, _):
        for m in range(4):
            base = ((4 * n + m) * block).astype(F32)
            spots = place[...]
            pick = jnp.concatenate([jnp.where(spots == mark + base, one, none) for mark in marks], axis=1)
            picked = dot(dext[...], pick)
            at = pl.ds(pl.multiple_of((4 * n + m) * block, block), block)
            box[at, :] = jnp.transpose(picked).astype(BF16)
        boxed(n).start()
        return 0

    steps = n_dev * cap // block // 4
    lax.fori_loop(0, steps, step, 0)
    for n in range(steps):
        boxed(n).wait()


def unpack_kernel(inbox, target, prof, left, right, side):
    total = inbox.shape[0]
    points = TX * TY
    lane = iota((8, 128), 1)
    mark = (lane == V).astype(F32).astype(BF16)
    acc = jnp.zeros((points, 128), F32)
    chunk = 1024
    for at in range(0, total, chunk):
        rows = inbox[at : at + chunk, :]
        slots = dot_t(mark, rows)[0:1, :].astype(jnp.int32)
        pick = (iota((points, chunk), 0) == slots).astype(F32).astype(BF16)
        acc = acc + dot(pick, rows)
    acc = jnp.where(iota((points, 128), 1) < V, acc, 0.0)
    for r in range(TX):
        goal = target[:, r, :]
        high = goal.astype(BF16).astype(F32)
        rest = goal - high
        side[...] = jnp.zeros((128, 128), F32)
        side[V : V + 3, :] = high
        side[V + 3 : V + 6, :] = rest
        part = acc[r * TY : (r + 1) * TY, :] + jnp.transpose(side[...])
        prof[r * TY : (r + 1) * TY, :] = part.astype(BF16)
        if r == 0:
            keep = part
    side[0:2, :] = keep[0:2, :]
    side[2:4, :] = part[0:2, :]
    side[4:16, :] = jnp.zeros((12, 128), F32)
    left[...] = side[0:16, :].astype(BF16)
    side[0:2, :] = keep[TY - 2 : TY, :]
    side[2:4, :] = part[TY - 2 : TY, :]
    right[...] = side[0:16, :].astype(BF16)


def turned(tile, shift):
    return tile if shift == 0 else pltpu.roll(tile, (-shift) % TY, 1)


def three(tile, beside, row):
    ends = turned(beside, 8 * row + 3)
    lane = iota((C, TY), 1)
    return (
        jnp.where(lane == 0, ends, turned(tile, -1)),
        tile,
        jnp.where(lane == TY - 1, ends, turned(tile, 1)),
    )


def wide_of(tiles):
    return jnp.concatenate(list(tiles), axis=1)


def step_kernel(own, first, second, wa, wat, wf, wb, wh, wht, sel, stress_out, pgrad, grads,
                ext, prof, unf, zs, zb, u1s, u2s, z2s, das, dzs, da1s, err_s, gb):
    patch = lax.axis_index("patch")
    body = lax.axis_index("body")
    odd_x = patch % 2 == 1
    odd_y = body % 2 == 1
    has_left = jnp.where(body > 0, 1.0, 0.0)
    has_right = jnp.where(body < lax.axis_size("body") - 1, 1.0, 0.0)
    has_up = jnp.where(patch > 0, 1.0, 0.0)
    has_down = jnp.where(patch < lax.axis_size("patch") - 1, 1.0, 0.0)
    ext[...] = jnp.zeros((128, 128), F32)
    goals = []
    one, two = first[...].astype(F32), second[...].astype(F32)
    sources = (
        jnp.where(odd_x, one, two) * has_up,
        own[...].astype(F32),
        jnp.where(odd_x, two, one) * has_down,
    )
    for row in range(ROWS):
        src, r = sources[row // TX], row % TX
        block = src[r * TY : (r + 1) * TY, :]
        one, two = src[256:288], src[288:320]
        left = jnp.where(odd_y, one, two)[16 + 2 * r : 18 + 2 * r] * has_left
        right = jnp.where(odd_y, two, one)[2 * r : 2 * r + 2] * has_right
        parts = (block[TY - 1 : TY], left[0:1], right[0:1], left[1:2], right[1:2], block[0:1])
        for n, part in enumerate(parts):
            ext[8 * row + n : 8 * row + n + 1, :] = part
        wide = jnp.transpose(block)
        prof[:, row * TY : (row + 1) * TY] = wide.astype(BF16)
        goals.append(wide[V : V + 8])
    wide = jnp.transpose(ext[...])
    prof[:, ROWS * TY : Q] = wide.astype(BF16)
    goal = wide_of(goals[1 : ROWS - 1] + [wide[V : V + 8]])
    goal = goal + jnp.concatenate([goal[3:8], goal[0:3]], axis=0)

    width = NA * TY
    lane = iota((8, width), 1)
    main = lane < (NA - 1) * TY
    spot = lane - (NA - 1) * TY
    row_at = jnp.where(main, lane // TY + 1, spot // 8)
    grid_x = patch * TX + row_at - TX
    inside_x = (grid_x >= 0) & (grid_x < lax.axis_size("patch") * TX)
    low = (spot % 8 == 3) & (body > 0)
    high = (spot % 8 == 2) & (body < lax.axis_size("body") - 1)
    ring = main | ((row_at >= 1) & (row_at <= ROWS - 2) & (low | high))
    mask = (ring & inside_x & (iota((8, width), 0) < 3)).astype(F32)

    def fill(zs_at, zb_at, p, which=(0, 1)):
        for n in which:
            u1 = dot(wa[2 * p + n], prof[...])
            z1 = (u1 + u1 * jnp.tanh(u1)).astype(BF16)
            for r in range(TX):
                u1s[2 * p + n, r] = u1[:, (TX + r) * TY : (TX + r + 1) * TY]
            beside = z1[:, ROWS * TY : Q]
            for row in range(ROWS):
                for m, part in enumerate(three(z1[:, row * TY : (row + 1) * TY], beside, row)):
                    at = (3 * row + m) * C
                    zs_at[n, at : at + C, :] = part
            for tap, shift in enumerate(BESIDE):
                zb_at[n, tap * C : (tap + 1) * C, :] = turned(beside, shift)

    def wall(zs_at, zb_at, p, which=range(NA)):
        spots = [(n, t) for n in range(2) for t in range(NA)]

        def taps(n, t):
            return zb_at[n] if t == NA - 1 else zs_at[n, 3 * C * t : 3 * C * t + KB, :]

        for g in which:
            pair = spots[2 * g : 2 * g + 2]
            both = dot(wf[...], wide_of([taps(n, t) for n, t in pair]))
            for m, (n, t) in enumerate(pair):
                u2 = both[:, TY * m : TY * (m + 1)]
                u2s[2 * p + n, t] = u2
                z1 = taps(n, t)[4 * C : 5 * C].astype(F32)
                act = z1 + (u2 + u2 * jnp.tanh(u2))
                rows = pl.ds(pl.multiple_of((2 * p + n) * C, C), C)
                z2s[t, rows, :] = act.astype(BF16)

    def forward(zs_at, zb_at, p):
        for kind, n in FORWARD:
            if kind == "F":
                fill(zs_at.at[2:4], zb_at.at[2:4], p + 1, (n,))
            else:
                wall(zs_at.at[0:2], zb_at.at[0:2], p, (n,))

    def forward_trip(q, _):
        zs_at = zs.at[pl.ds(2 * TRIP * q + 2, 2 * TRIP + 2)]
        zb_at = zb.at[pl.ds(2 * TRIP * q + 2, 2 * TRIP + 2)]
        for m in range(TRIP):
            at = slice(2 * m, 2 * m + 4)
            forward(zs_at.at[at], zb_at.at[at], TRIP * q + 1 + m)
        return 0

    fill(zs.at[0:2], zb.at[0:2], 0)
    forward(zs.at[0:4], zb.at[0:4], 0)
    lax.fori_loop(0, (H // 2 - 2) // TRIP, forward_trip, 0)
    wall(zs.at[H - 2 : H], zb.at[H - 2 : H], H // 2 - 1)
    stress = wide_of(
        [dot(wh[...], wide_of([z2s[t] for t in range(n, min(n + 2, NA))])) for n in range(0, NA, 2)]
    )
    for r in range(TX):
        stress_out[:, r, :] = stress[0:3, (1 + r) * TY : (2 + r) * TY]
    err = ((stress - goal) * mask).astype(BF16)
    err_s[...] = err
    grad_h = dot_t(err[:, TY : 3 * TY], wide_of([z2s[1], z2s[2]]))
    unf[...] = dot(sel[...], prof[:, TX * TY : 2 * TX * TY]).astype(BF16).reshape(H, 16, TX * TY)
    gb[...] = jnp.zeros_like(gb)

    def third(das_at, dz_at, p, which=(0, 1)):
        for n in which:
            h = 2 * p + n
            u2 = wide_of([u2s[h, t] for t in range(NA)])
            t2 = jnp.tanh(u2)
            dz2 = dot(wht[h], err_s[...])
            da2 = (dz2 * ((1.0 + t2) * (1.0 + u2 * (1.0 - t2)))).astype(BF16)
            beside = da2[:, (NA - 1) * TY : width]
            for t in range(NA - 1):
                for m, part in enumerate(three(da2[:, t * TY : (t + 1) * TY], beside, t + 1)):
                    at = (3 * t + m) * C
                    das_at[n, at : at + C, :] = part
            dz_at[n] = dz2[:, TY : 3 * TY]

    def fifth(das_at, p):
        spots = [(n, t) for n in range(2) for t in (1, 2)]
        mids = [das_at[n, (3 * t + 1) * C : (3 * t + 2) * C, :] for n, t in spots]
        kept = [zs[2 * p + n, 3 * C * t : 3 * C * t + KB, :] for n, t in spots]
        gb[...] += dot_t(wide_of(mids), wide_of(kept))

    def fourth(das_at, dz_at, p, grad_a, which=(0, 1)):
        for n in which:
            h = 2 * p + n
            conv = dot(wb[...], wide_of([das_at[n, 3 * C * t : 3 * C * t + KB, :] for t in range(TX)]))
            u1 = wide_of([u1s[h, r] for r in range(TX)])
            t1 = jnp.tanh(u1)
            da1 = ((dz_at[n] + conv) * ((1.0 + t1) * (1.0 + u1 * (1.0 - t1)))).astype(BF16)
            rows = pl.ds(pl.multiple_of(h * C, C), C)
            for r in range(TX):
                da1s[r, rows, :] = da1[:, r * TY : (r + 1) * TY]
            grad_a = grad_a + dot_t(unf[h], da1)
        return grad_a

    def backward(das_at, dz_at, p, grad_a):
        for kind, n in BACKWARD:
            if kind == "T":
                third(das_at.at[2:4], dz_at.at[2:4], p + 1, (n,))
            elif kind == "G":
                fifth(das_at.at[0:2], p)
            else:
                grad_a = fourth(das_at.at[0:2], dz_at.at[0:2], p, grad_a, (n,))
        return grad_a

    def backward_trip(q, grad_a):
        das_at = das.at[pl.ds(2 * TRIP * q + 2, 2 * TRIP + 2)]
        dz_at = dzs.at[pl.ds(2 * TRIP * q + 2, 2 * TRIP + 2)]
        for m in range(TRIP):
            at = slice(2 * m, 2 * m + 4)
            grad_a = backward(das_at.at[at], dz_at.at[at], TRIP * q + 1 + m, grad_a)
        return grad_a

    third(das.at[0:2], dzs.at[0:2], 0)
    grad_a = backward(das.at[0:4], dzs.at[0:4], 0, jnp.zeros((16, C), F32))
    grad_a = lax.fori_loop(0, (H // 2 - 2) // TRIP, backward_trip, grad_a)
    fifth(das.at[H - 2 : H], H // 2 - 1)
    grad_a = fourth(das.at[H - 2 : H], dzs.at[H - 2 : H], H // 2 - 1, grad_a)
    grad_a = jnp.concatenate([grad_a, jnp.zeros((16, 128 - C), F32)], axis=1)
    parts = [grad_h[0:3, t * 128 : (t + 1) * 128] for t in range(H * C // 128)]
    small = jnp.concatenate(parts + [grad_a, jnp.zeros((SMALL - GH - 16, 128), F32)], axis=0)
    grad_b = jnp.concatenate([gb[...], jnp.zeros((C, KT * 128 - KB), F32)], axis=1)
    blocks = [grad_b[8 * i : 8 * i + 8, 128 * t : 128 * (t + 1)] for t in range(KT) for i in range(C // 8)]
    blocks += [small[8 * i : 8 * i + 8] for i in range(SMALL // 8)]
    for n, block in enumerate(blocks):
        for i in range(4):
            dev, k = divmod(4 * n + i, 3)
            grads[dev, :, 128 * k : 128 * (k + 1)] = block[2 * i : 2 * i + 2]
    back = dot(wat[...], wide_of([da1s[r] for r in range(TX)]))
    for r in range(TX):
        pgrad[:, r, :] = back[0:V, r * TY : (r + 1) * TY]


def spread_kernel(sums, grad_a, grad_b, grad_h):
    def rows_at(first, count):
        pairs = []
        for j in range(first // 2, (first + count) // 2):
            dev, k = divmod(j, 3)
            pairs.append(sums[dev, :, 128 * k : 128 * (k + 1)].astype(F32))
        return jnp.concatenate(pairs, axis=0)

    for t in range(KT):
        tall = jnp.transpose(rows_at(t * C, C))
        count = min(128, KB - 128 * t)
        grad_b[128 * t : 128 * t + count, :] = tall[0:count, :]
    small = rows_at(KT * C, SMALL)
    for t in range(H * C // 128):
        grad_h[:, t * 128 : (t + 1) * 128] = small[3 * t : 3 * t + 3]
    for k in range(3):
        for f in range(F):
            n = GH + k * F + f
            grad_a[f, k : k + 1, :] = small[n : n + 1, 0:C]


def call(kernel, limit, out_shape, scratch=(), space=pltpu.VMEM, flags=None):
    near = pl.BlockSpec(memory_space=space)

    def run(*operands):
        return pl.pallas_call(
            kernel,
            out_shape=out_shape,
            in_specs=[near] * len(operands),
            out_specs=jax.tree.map(lambda _: near, out_shape),
            scratch_shapes=list(scratch),
            compiler_params=pltpu.CompilerParams(vmem_limit_bytes=limit * MIB, flags=flags),
        )(*operands)

    return run


def shape(dims, kind):
    return jax.ShapeDtypeStruct(dims, kind)


def exchange(blocks):
    return lax.all_to_all(blocks, AXES, split_axis=0, concat_axis=0, tiled=True)


def trades(count):
    inner = [(i, i ^ 1) for i in range(count)]
    outer = [(i, i - 1 + 2 * (i % 2)) for i in range(1, count - 1)] + [(0, 0), (count - 1, count - 1)]
    return inner, outer


def shards(donors, owner, slot, target, weight_a, weight_b, weight_h):
    n_patch = lax.axis_size("patch")
    n_body = lax.axis_size("body")
    n_dev = n_patch * n_body
    rows = donors.shape[1]
    cap = 2 * rows // n_dev
    outbox = call(
        functools.partial(pack_kernel, cap),
        60,
        shape((n_dev * cap, 128), BF16),
        [
            pltpu.VMEM((128, rows), BF16),
            pltpu.VMEM((1, rows), jnp.int32),
            pltpu.VMEM((1, rows), jnp.int32),
            pltpu.VMEM((rows // 128, 1, 128), F32),
            pltpu.VMEM((rows, 128), F32),
            pltpu.VMEM((n_dev * cap, 128), BF16),
            pltpu.SemaphoreType.DMA((3 + n_dev * cap // 1024,)),
        ],
        pltpu.HBM,
    )(donors, owner.reshape(1, rows), slot.reshape(1, rows))
    inbox = exchange(outbox.reshape(n_dev, cap, 128)).reshape(n_dev * cap, 128)

    half = jnp.asarray(0.5, BF16)
    heights = jnp.arange(H)
    reach = heights[None, :, None] + 2 * (jnp.arange(3)[:, None, None] - 1) == heights[None, None, :]
    band = jnp.einsum("khg,kfc->hcgf", reach.astype(BF16), weight_a).reshape(H * C, V)
    band = jnp.pad(band, ((0, 0), (0, 128 - V)))
    wa = (band * half).reshape(H, C, 128)
    wat = jnp.transpose(band)
    wf = jnp.transpose(weight_b, (2, 0, 1)).reshape(C, KB) * half
    wb = jnp.transpose(weight_b[::-1], (1, 0, 2)).reshape(C, KB) * half
    wh = jnp.pad(jnp.transpose(weight_h), ((0, 5), (0, 0)))
    wht = (jnp.pad(weight_h, ((0, 0), (0, 5))) * half).reshape(H, C, 8)
    line = jnp.arange(16)
    want = (heights[:, None] + 2 * (line[None, :] // F - 1)) * F + line[None, :] % F
    sel = (want[:, :, None] == jnp.arange(128)[None, None, :]) & (want >= 0)[:, :, None]
    sel = sel & (want < V)[:, :, None] & (line < 15)[None, :, None]
    sel = sel.astype(BF16).reshape(H * 16, 128)

    inbox, wa, wat, wf, wb, wh, wht, sel = lax.optimization_barrier(
        (inbox, wa, wat, wf, wb, wh, wht, sel)
    )
    prof, left, right = call(
        unpack_kernel,
        8,
        (shape((TX * TY, 128), BF16), shape((16, 128), BF16), shape((16, 128), BF16)),
        [pltpu.VMEM((128, 128), F32)],
    )(inbox, jnp.transpose(target, (2, 0, 1)))
    edges = jnp.concatenate([left, right], axis=0)
    sides = [lax.ppermute(edges, "body", trade) for trade in trades(n_body)]
    tile = jnp.concatenate([prof] + sides, axis=0)
    first, second = [lax.ppermute(tile, "patch", trade) for trade in trades(n_patch)]

    stress, pgrad, grads = call(
        step_kernel,
        46,
        (shape((3, TX, TY), F32), shape((V, TX, TY), F32), shape((n_dev, 2, 384), F32)),
        [
            pltpu.VMEM((128, 128), F32),
            pltpu.VMEM((128, Q), BF16),
            pltpu.VMEM((H, 16, TX * TY), BF16),
            pltpu.VMEM((H, 3 * ROWS * C, TY), BF16),
            pltpu.VMEM((H, KB, TY), BF16),
            pltpu.VMEM((H, TX, C, TY), F32),
            pltpu.VMEM((H, NA, C, TY), F32),
            pltpu.VMEM((NA, H * C, TY), BF16),
            pltpu.VMEM((H, 3 * (NA - 1) * C, TY), BF16),
            pltpu.VMEM((H, C, TX * TY), F32),
            pltpu.VMEM((TX, H * C, TY), BF16),
            pltpu.VMEM((8, NA * TY), BF16),
            pltpu.VMEM((C, KB), F32),
        ],
    )(tile, first, second, wa, wat, wf, wb, wh, wht, sel)
    scale = 1.0 / jnp.sqrt(jnp.float32(TX * TY * n_dev))
    total = (jnp.sum(exchange(grads), axis=0) * scale).astype(BF16)
    sums = exchange(jnp.broadcast_to(total[None], (n_dev, 2, 384)))
    grad_a, grad_b, grad_h = call(
        spread_kernel,
        6,
        (shape((F, 3, C), F32), shape((KB, C), F32), shape((3, H * C), F32)),
    )(sums)
    return (
        jnp.transpose(stress, (1, 2, 0)),
        pgrad,
        jnp.transpose(grad_a, (1, 0, 2)),
        grad_b.reshape(9, C, C),
        jnp.transpose(grad_h),
    )


def solution(mesh):
    placed = (
        P(None, ("patch", "body")),
        P(("patch", "body"), None),
        P(("patch", "body")),
        P("patch", "body", None),
        P(),
        P(),
        P(),
    )
    return jax.shard_map(
        shards,
        mesh=mesh,
        in_specs=placed,
        out_specs=(P("patch", "body", None), P(None, "patch", "body"), P(), P(), P()),
        check_vma=False,
    )
```

```python
import functools

import jax
import jax.numpy as jnp
from jax import lax
from jax.experimental import pallas as pl
from jax.experimental.pallas import tpu as pltpu
from jax.sharding import PartitionSpec as P

F32 = jnp.float32
BF16 = jnp.bfloat16
AXES = ("patch", "body")
C = 96
H = 24
F = 5
V = H * F
TX = 2
TY = 128
ROWS = TX + 4
NZ = ROWS + 1
NA = ROWS - 1
Q = NZ * TY
KB = 9 * C
BESIDE = tuple((di - 1) * 8 + (dj - 1) * 2 for di in range(3) for dj in range(3))
KT = -(-KB // 128)
GH = 3 * H * C // 128
SMALL = 768 - KT * C
COLS = (((1,), (1,)), ((), ()))
MIB = 1024 * 1024
TRIP = 10
FORWARD = (("F", 0), ("W", 0), ("F", 1), ("W", 1), ("W", 2), ("W", 3), ("W", 4))
BACKWARD = (("T", 0), ("B", 0), ("T", 1), ("G", 0), ("B", 1))


def dot(a, b):
    return jnp.dot(a, b, preferred_element_type=F32)


def dot_t(a, b):
    return lax.dot_general(a, b, COLS, preferred_element_type=F32)


def iota(shape, dim):
    return lax.broadcasted_iota(jnp.int32, shape, dim)


def pack_kernel(cap, donors_far, owner_far, slot_far, out, dext, owner, slot, ranked, place, box, sems):
    rows = donors_far.shape[1]
    n_dev = 128
    own_copy = pltpu.make_async_copy(owner_far, owner, sems.at[0])
    slot_copy = pltpu.make_async_copy(slot_far, slot, sems.at[1])
    donor_copy = pltpu.make_async_copy(donors_far, dext.at[0:V], sems.at[2])
    own_copy.start()
    slot_copy.start()
    donor_copy.start()
    part = 256
    upper = (iota((part, part), 0) < iota((part, part), 1)).astype(F32).astype(BF16)
    own_copy.wait()

    def count(q, carry):
        for n in (2 * q, 2 * q + 1):
            dest = owner[:, pl.ds(pl.multiple_of(n * part, part), part)]
            hit = (iota((n_dev, part), 0) == dest).astype(F32)
            before = dot(hit.astype(BF16), upper) + carry
            rank = jnp.sum(before * hit, axis=0, keepdims=True)
            spot = (dest * cap).astype(F32) + rank
            ranked[2 * n] = spot[:, 0:128]
            ranked[2 * n + 1] = spot[:, 128:256]
            carry = carry + jnp.sum(hit, axis=1, keepdims=True)
        return carry

    lax.fori_loop(0, rows // part // 2, count, jnp.zeros((n_dev, 1), F32))
    block = 256
    tall = jnp.transpose(jnp.concatenate([ranked[n] for n in range(rows // 128)], axis=0))
    for n in range(rows // 128):
        place[n * 128 : (n + 1) * 128, :] = jnp.broadcast_to(tall[:, n : n + 1], (128, 128))
    slot_copy.wait()
    pad = iota((8, rows), 0)
    dext[V : V + 8, :] = jnp.where(pad == 0, slot[...], 0).astype(F32).astype(BF16)
    donor_copy.wait()
    marks = [(iota((1, 128), 1) + 128 * t).astype(F32) for t in range(2)]
    one, none = jnp.asarray(1.0, BF16), jnp.asarray(0.0, BF16)

    def boxed(n):
        at = pl.ds(pl.multiple_of(n * 4 * block, 4 * block), 4 * block)
        return pltpu.make_async_copy(box.at[at], out.at[at], sems.at[3 + n])

    def step(n, _):
        for m in range(4):
            base = ((4 * n + m) * block).astype(F32)
            spots = place[...]
            pick = jnp.concatenate([jnp.where(spots == mark + base, one, none) for mark in marks], axis=1)
            picked = dot(dext[...], pick)
            at = pl.ds(pl.multiple_of((4 * n + m) * block, block), block)
            box[at, :] = jnp.transpose(picked).astype(BF16)
        boxed(n).start()
        return 0

    steps = n_dev * cap // block // 4
    lax.fori_loop(0, steps, step, 0)
    for n in range(steps):
        boxed(n).wait()


def unpack_kernel(inbox, target, prof, left, right, side):
    total = inbox.shape[0]
    points = TX * TY
    lane = iota((8, 128), 1)
    mark = (lane == V).astype(F32).astype(BF16)
    acc = jnp.zeros((points, 128), F32)
    chunk = 1024
    for at in range(0, total, chunk):
        rows = inbox[at : at + chunk, :]
        slots = dot_t(mark, rows)[0:1, :].astype(jnp.int32)
        pick = (iota((points, chunk), 0) == slots).astype(F32).astype(BF16)
        acc = acc + dot(pick, rows)
    acc = jnp.where(iota((points, 128), 1) < V, acc, 0.0)
    for r in range(TX):
        goal = target[:, r, :]
        high = goal.astype(BF16).astype(F32)
        rest = goal - high
        side[...] = jnp.zeros((128, 128), F32)
        side[V : V + 3, :] = high
        side[V + 3 : V + 6, :] = rest
        part = acc[r * TY : (r + 1) * TY, :] + jnp.transpose(side[...])
        prof[r * TY : (r + 1) * TY, :] = part.astype(BF16)
        if r == 0:
            keep = part
    side[0:2, :] = keep[0:2, :]
    side[2:4, :] = part[0:2, :]
    side[4:16, :] = jnp.zeros((12, 128), F32)
    left[...] = side[0:16, :].astype(BF16)
    side[0:2, :] = keep[TY - 2 : TY, :]
    side[2:4, :] = part[TY - 2 : TY, :]
    right[...] = side[0:16, :].astype(BF16)


def turned(tile, shift):
    return tile if shift == 0 else pltpu.roll(tile, (-shift) % TY, 1)


def three(tile, beside, row):
    ends = turned(beside, 8 * row + 3)
    lane = iota((C, TY), 1)
    return (
        jnp.where(lane == 0, ends, turned(tile, -1)),
        tile,
        jnp.where(lane == TY - 1, ends, turned(tile, 1)),
    )


def wide_of(tiles):
    return jnp.concatenate(list(tiles), axis=1)


def step_kernel(own, first, second, wa, wat, wf, wb, wh, wht, sel, stress_out, pgrad, grads,
                ext, prof, unf, zs, zb, u1s, u2s, z2s, das, dzs, da1s, err_s, gb):
    patch = lax.axis_index("patch")
    body = lax.axis_index("body")
    odd_x = patch % 2 == 1
    odd_y = body % 2 == 1
    has_left = jnp.where(body > 0, 1.0, 0.0)
    has_right = jnp.where(body < lax.axis_size("body") - 1, 1.0, 0.0)
    has_up = jnp.where(patch > 0, 1.0, 0.0)
    has_down = jnp.where(patch < lax.axis_size("patch") - 1, 1.0, 0.0)
    ext[...] = jnp.zeros((128, 128), F32)
    goals = []
    one, two = first[...].astype(F32), second[...].astype(F32)
    sources = (
        jnp.where(odd_x, one, two) * has_up,
        own[...].astype(F32),
        jnp.where(odd_x, two, one) * has_down,
    )
    for row in range(ROWS):
        src, r = sources[row // TX], row % TX
        block = src[r * TY : (r + 1) * TY, :]
        one, two = src[256:288], src[288:320]
        left = jnp.where(odd_y, one, two)[16 + 2 * r : 18 + 2 * r] * has_left
        right = jnp.where(odd_y, two, one)[2 * r : 2 * r + 2] * has_right
        parts = (block[TY - 1 : TY], left[0:1], right[0:1], left[1:2], right[1:2], block[0:1])
        for n, part in enumerate(parts):
            ext[8 * row + n : 8 * row + n + 1, :] = part
        wide = jnp.transpose(block)
        prof[:, row * TY : (row + 1) * TY] = wide.astype(BF16)
        goals.append(wide[V : V + 8])
    wide = jnp.transpose(ext[...])
    prof[:, ROWS * TY : Q] = wide.astype(BF16)
    goal = wide_of(goals[1 : ROWS - 1] + [wide[V : V + 8]])
    goal = goal + jnp.concatenate([goal[3:8], goal[0:3]], axis=0)

    width = NA * TY
    lane = iota((8, width), 1)
    main = lane < (NA - 1) * TY
    spot = lane - (NA - 1) * TY
    row_at = jnp.where(main, lane // TY + 1, spot // 8)
    grid_x = patch * TX + row_at - TX
    inside_x = (grid_x >= 0) & (grid_x < lax.axis_size("patch") * TX)
    low = (spot % 8 == 3) & (body > 0)
    high = (spot % 8 == 2) & (body < lax.axis_size("body") - 1)
    ring = main | ((row_at >= 1) & (row_at <= ROWS - 2) & (low | high))
    mask = (ring & inside_x & (iota((8, width), 0) < 3)).astype(F32)

    def fill(zs_at, zb_at, p, which=(0, 1)):
        for n in which:
            u1 = dot(wa[2 * p + n], prof[...])
            z1 = (u1 + u1 * jnp.tanh(u1)).astype(BF16)
            for r in range(TX):
                u1s[2 * p + n, r] = u1[:, (TX + r) * TY : (TX + r + 1) * TY]
            beside = z1[:, ROWS * TY : Q]
            for row in range(ROWS):
                for m, part in enumerate(three(z1[:, row * TY : (row + 1) * TY], beside, row)):
                    at = (3 * row + m) * C
                    zs_at[n, at : at + C, :] = part
            for tap, shift in enumerate(BESIDE):
                zb_at[n, tap * C : (tap + 1) * C, :] = turned(beside, shift)

    def wall(zs_at, zb_at, p, which=range(NA)):
        spots = [(n, t) for n in range(2) for t in range(NA)]

        def taps(n, t):
            return zb_at[n] if t == NA - 1 else zs_at[n, 3 * C * t : 3 * C * t + KB, :]

        for g in which:
            pair = spots[2 * g : 2 * g + 2]
            both = dot(wf[...], wide_of([taps(n, t) for n, t in pair]))
            for m, (n, t) in enumerate(pair):
                u2 = both[:, TY * m : TY * (m + 1)]
                u2s[2 * p + n, t] = u2
                z1 = taps(n, t)[4 * C : 5 * C].astype(F32)
                act = z1 + (u2 + u2 * jnp.tanh(u2))
                rows = pl.ds(pl.multiple_of((2 * p + n) * C, C), C)
                z2s[t, rows, :] = act.astype(BF16)

    def forward(zs_at, zb_at, p):
        for kind, n in FORWARD:
            if kind == "F":
                fill(zs_at.at[2:4], zb_at.at[2:4], p + 1, (n,))
            else:
                wall(zs_at.at[0:2], zb_at.at[0:2], p, (n,))

    def forward_trip(q, _):
        zs_at = zs.at[pl.ds(2 * TRIP * q + 2, 2 * TRIP + 2)]
        zb_at = zb.at[pl.ds(2 * TRIP * q + 2, 2 * TRIP + 2)]
        for m in range(TRIP):
            at = slice(2 * m, 2 * m + 4)
            forward(zs_at.at[at], zb_at.at[at], TRIP * q + 1 + m)
        return 0

    fill(zs.at[0:2], zb.at[0:2], 0)
    forward(zs.at[0:4], zb.at[0:4], 0)
    lax.fori_loop(0, (H // 2 - 2) // TRIP, forward_trip, 0)
    wall(zs.at[H - 2 : H], zb.at[H - 2 : H], H // 2 - 1)
    stress = wide_of(
        [dot(wh[...], wide_of([z2s[t] for t in range(n, min(n + 2, NA))])) for n in range(0, NA, 2)]
    )
    for r in range(TX):
        stress_out[:, r, :] = stress[0:3, (1 + r) * TY : (2 + r) * TY]
    err = ((stress - goal) * mask).astype(BF16)
    err_s[...] = err
    grad_h = dot_t(err[:, TY : 3 * TY], wide_of([z2s[1], z2s[2]]))
    unf[...] = dot(sel[...], prof[:, TX * TY : 2 * TX * TY]).astype(BF16).reshape(H, 16, TX * TY)
    gb[...] = jnp.zeros_like(gb)

    def third(das_at, dz_at, p, which=(0, 1)):
        for n in which:
            h = 2 * p + n
            u2 = wide_of([u2s[h, t] for t in range(NA)])
            t2 = jnp.tanh(u2)
            dz2 = dot(wht[h], err_s[...])
            da2 = (dz2 * ((1.0 + t2) * (1.0 + u2 * (1.0 - t2)))).astype(BF16)
            beside = da2[:, (NA - 1) * TY : width]
            for t in range(NA - 1):
                for m, part in enumerate(three(da2[:, t * TY : (t + 1) * TY], beside, t + 1)):
                    at = (3 * t + m) * C
                    das_at[n, at : at + C, :] = part
            dz_at[n] = dz2[:, TY : 3 * TY]

    def fifth(das_at, p):
        spots = [(n, t) for n in range(2) for t in (1, 2)]
        mids = [das_at[n, (3 * t + 1) * C : (3 * t + 2) * C, :] for n, t in spots]
        kept = [zs[2 * p + n, 3 * C * t : 3 * C * t + KB, :] for n, t in spots]
        gb[...] += dot_t(wide_of(mids), wide_of(kept))

    def fourth(das_at, dz_at, p, grad_a, which=(0, 1)):
        for n in which:
            h = 2 * p + n
            conv = dot(wb[...], wide_of([das_at[n, 3 * C * t : 3 * C * t + KB, :] for t in range(TX)]))
            u1 = wide_of([u1s[h, r] for r in range(TX)])
            t1 = jnp.tanh(u1)
            da1 = ((dz_at[n] + conv) * ((1.0 + t1) * (1.0 + u1 * (1.0 - t1)))).astype(BF16)
            rows = pl.ds(pl.multiple_of(h * C, C), C)
            for r in range(TX):
                da1s[r, rows, :] = da1[:, r * TY : (r + 1) * TY]
            grad_a = grad_a + dot_t(unf[h], da1)
        return grad_a

    def backward(das_at, dz_at, p, grad_a):
        for kind, n in BACKWARD:
            if kind == "T":
                third(das_at.at[2:4], dz_at.at[2:4], p + 1, (n,))
            elif kind == "G":
                fifth(das_at.at[0:2], p)
            else:
                grad_a = fourth(das_at.at[0:2], dz_at.at[0:2], p, grad_a, (n,))
        return grad_a

    def backward_trip(q, grad_a):
        das_at = das.at[pl.ds(2 * TRIP * q + 2, 2 * TRIP + 2)]
        dz_at = dzs.at[pl.ds(2 * TRIP * q + 2, 2 * TRIP + 2)]
        for m in range(TRIP):
            at = slice(2 * m, 2 * m + 4)
            grad_a = backward(das_at.at[at], dz_at.at[at], TRIP * q + 1 + m, grad_a)
        return grad_a

    third(das.at[0:2], dzs.at[0:2], 0)
    grad_a = backward(das.at[0:4], dzs.at[0:4], 0, jnp.zeros((16, C), F32))
    grad_a = lax.fori_loop(0, (H // 2 - 2) // TRIP, backward_trip, grad_a)
    fifth(das.at[H - 2 : H], H // 2 - 1)
    grad_a = fourth(das.at[H - 2 : H], dzs.at[H - 2 : H], H // 2 - 1, grad_a)
    grad_a = jnp.concatenate([grad_a, jnp.zeros((16, 128 - C), F32)], axis=1)
    parts = [grad_h[0:3, t * 128 : (t + 1) * 128] for t in range(H * C // 128)]
    small = jnp.concatenate(parts + [grad_a, jnp.zeros((SMALL - GH - 16, 128), F32)], axis=0)
    grad_b = jnp.concatenate([gb[...], jnp.zeros((C, KT * 128 - KB), F32)], axis=1)
    blocks = [grad_b[8 * i : 8 * i + 8, 128 * t : 128 * (t + 1)] for t in range(KT) for i in range(C // 8)]
    blocks += [small[8 * i : 8 * i + 8] for i in range(SMALL // 8)]
    for n, block in enumerate(blocks):
        for i in range(4):
            dev, k = divmod(4 * n + i, 3)
            grads[dev, :, 128 * k : 128 * (k + 1)] = block[2 * i : 2 * i + 2]
    back = dot(wat[...], wide_of([da1s[r] for r in range(TX)]))
    for r in range(TX):
        pgrad[:, r, :] = back[0:V, r * TY : (r + 1) * TY]


def spread_kernel(sums, grad_a, grad_b, grad_h):
    def rows_at(first, count):
        pairs = []
        for j in range(first // 2, (first + count) // 2):
            dev, k = divmod(j, 3)
            pairs.append(sums[dev, :, 128 * k : 128 * (k + 1)].astype(F32))
        return jnp.concatenate(pairs, axis=0)

    for t in range(KT):
        tall = jnp.transpose(rows_at(t * C, C))
        count = min(128, KB - 128 * t)
        grad_b[128 * t : 128 * t + count, :] = tall[0:count, :]
    small = rows_at(KT * C, SMALL)
    for t in range(H * C // 128):
        grad_h[:, t * 128 : (t + 1) * 128] = small[3 * t : 3 * t + 3]
    for k in range(3):
        for f in range(F):
            n = GH + k * F + f
            grad_a[f, k : k + 1, :] = small[n : n + 1, 0:C]


def call(kernel, limit, out_shape, scratch=(), space=pltpu.VMEM, flags=None):
    near = pl.BlockSpec(memory_space=space)

    def run(*operands):
        return pl.pallas_call(
            kernel,
            out_shape=out_shape,
            in_specs=[near] * len(operands),
            out_specs=jax.tree.map(lambda _: near, out_shape),
            scratch_shapes=list(scratch),
            compiler_params=pltpu.CompilerParams(vmem_limit_bytes=limit * MIB, flags=flags),
        )(*operands)

    return run


def shape(dims, kind):
    return jax.ShapeDtypeStruct(dims, kind)


def exchange(blocks):
    return lax.all_to_all(blocks, AXES, split_axis=0, concat_axis=0, tiled=True)


def trades(count):
    inner = [(i, i ^ 1) for i in range(count)]
    outer = [(i, i - 1 + 2 * (i % 2)) for i in range(1, count - 1)] + [(0, 0), (count - 1, count - 1)]
    return inner, outer


def shards(donors, owner, slot, target, weight_a, weight_b, weight_h):
    n_patch = lax.axis_size("patch")
    n_body = lax.axis_size("body")
    n_dev = n_patch * n_body
    rows = donors.shape[1]
    cap = 2 * rows // n_dev
    outbox = call(
        functools.partial(pack_kernel, cap),
        60,
        shape((n_dev * cap, 128), BF16),
        [
            pltpu.VMEM((128, rows), BF16),
            pltpu.VMEM((1, rows), jnp.int32),
            pltpu.VMEM((1, rows), jnp.int32),
            pltpu.VMEM((rows // 128, 1, 128), F32),
            pltpu.VMEM((rows, 128), F32),
            pltpu.VMEM((n_dev * cap, 128), BF16),
            pltpu.SemaphoreType.DMA((3 + n_dev * cap // 1024,)),
        ],
        pltpu.HBM,
    )(donors, owner.reshape(1, rows), slot.reshape(1, rows))
    inbox = exchange(outbox.reshape(n_dev, cap, 128)).reshape(n_dev * cap, 128)

    half = jnp.asarray(0.5, BF16)
    heights = jnp.arange(H)
    reach = heights[None, :, None] + 2 * (jnp.arange(3)[:, None, None] - 1) == heights[None, None, :]
    band = jnp.einsum("khg,kfc->hcgf", reach.astype(BF16), weight_a).reshape(H * C, V)
    band = jnp.pad(band, ((0, 0), (0, 128 - V)))
    wa = (band * half).reshape(H, C, 128)
    wat = jnp.transpose(band)
    wf = jnp.transpose(weight_b, (2, 0, 1)).reshape(C, KB) * half
    wb = jnp.transpose(weight_b[::-1], (1, 0, 2)).reshape(C, KB) * half
    wh = jnp.pad(jnp.transpose(weight_h), ((0, 5), (0, 0)))
    wht = (jnp.pad(weight_h, ((0, 0), (0, 5))) * half).reshape(H, C, 8)
    line = jnp.arange(16)
    want = (heights[:, None] + 2 * (line[None, :] // F - 1)) * F + line[None, :] % F
    sel = (want[:, :, None] == jnp.arange(128)[None, None, :]) & (want >= 0)[:, :, None]
    sel = sel & (want < V)[:, :, None] & (line < 15)[None, :, None]
    sel = sel.astype(BF16).reshape(H * 16, 128)

    inbox, wa, wat, wf, wb, wh, wht, sel = lax.optimization_barrier(
        (inbox, wa, wat, wf, wb, wh, wht, sel)
    )
    prof, left, right = call(
        unpack_kernel,
        8,
        (shape((TX * TY, 128), BF16), shape((16, 128), BF16), shape((16, 128), BF16)),
        [pltpu.VMEM((128, 128), F32)],
    )(inbox, jnp.transpose(target, (2, 0, 1)))
    edges = jnp.concatenate([left, right], axis=0)
    sides = [lax.ppermute(edges, "body", trade) for trade in trades(n_body)]
    tile = jnp.concatenate([prof] + sides, axis=0)
    first, second = [lax.ppermute(tile, "patch", trade) for trade in trades(n_patch)]

    stress, pgrad, grads = call(
        step_kernel,
        46,
        (shape((3, TX, TY), F32), shape((V, TX, TY), F32), shape((n_dev, 2, 384), F32)),
        [
            pltpu.VMEM((128, 128), F32),
            pltpu.VMEM((128, Q), BF16),
            pltpu.VMEM((H, 16, TX * TY), BF16),
            pltpu.VMEM((H, 3 * ROWS * C, TY), BF16),
            pltpu.VMEM((H, KB, TY), BF16),
            pltpu.VMEM((H, TX, C, TY), F32),
            pltpu.VMEM((H, NA, C, TY), F32),
            pltpu.VMEM((NA, H * C, TY), BF16),
            pltpu.VMEM((H, 3 * (NA - 1) * C, TY), BF16),
            pltpu.VMEM((H, C, TX * TY), F32),
            pltpu.VMEM((TX, H * C, TY), BF16),
            pltpu.VMEM((8, NA * TY), BF16),
            pltpu.VMEM((C, KB), F32),
        ],
    )(tile, first, second, wa, wat, wf, wb, wh, wht, sel)
    scale = 1.0 / jnp.sqrt(jnp.float32(TX * TY * n_dev))
    total = (jnp.sum(exchange(grads), axis=0) * scale).astype(BF16)
    sums = exchange(jnp.broadcast_to(total[None], (n_dev, 2, 384)))
    grad_a, grad_b, grad_h = call(
        spread_kernel,
        6,
        (shape((F, 3, C), F32), shape((KB, C), F32), shape((3, H * C), F32)),
    )(sums)
    return (
        jnp.transpose(stress, (1, 2, 0)),
        pgrad,
        jnp.transpose(grad_a, (1, 0, 2)),
        grad_b.reshape(9, C, C),
        jnp.transpose(grad_h),
    )


def solution(mesh):
    placed = (
        P(None, ("patch", "body")),
        P(("patch", "body"), None),
        P(("patch", "body")),
        P("patch", "body", None),
        P(),
        P(),
        P(),
    )
    return jax.shard_map(
        shards,
        mesh=mesh,
        in_specs=placed,
        out_specs=(P("patch", "body", None), P(None, "patch", "body"), P(), P(), P()),
        check_vma=False,
    )
```
